32 devices in a mesh: grp: 4 (over x, core), sub: 8 (over z, y).
Axes of the slice: x: 2, y: 2, z: 4, core: 2. Of those that a mesh axis runs over, the one named last changes fastest.
Arguments:
- shell_state: float32 [2, 48, 262144], P(None, None, ('grp', 'sub')), may hold values from -6 to 6
- source: bfloat16 [2, 256, 16, 768], P(None, ('grp', 'sub')), may hold values from -6 to 6
- knockdown: bfloat16 [256, 16, 768], P(('grp', 'sub')), may hold values from 0.29882812 to 3
- orient: int32 [256, 48], P(('grp', 'sub')), may hold values from 0 to 3
- active: int32 [256], P(('grp', 'sub')), may hold values from 24 to 48
- point_owner: int32 [256, 64], P(('grp', 'sub')), may hold values from 0 to 31, as said below
- owner_nodes: int32 [32, 32, 32], P(('grp', 'sub')), may hold values from -1 to 8191, as said below
Outputs:
- adjoint: float32 [2, 256, 16, 768], P(None, ('grp', 'sub'))
- shell_force: float32 [2, 48, 262144], P(None, None, ('grp', 'sub'))
The draws below stay inside these ranges and needn't reach their ends.
Inputs may be any that keep to these rules, and one draw needn't show every extreme that they name: `point_owner`: within every block of boundary columns (see the steps), no owner appears more than 32 times, and in every draw one owner, the same for all blocks, appears exactly 32 times in each block. owner_nodes[o, d, r] is the local node of the column of block d with owner o that has r earlier such columns, and -1 for r at or beyond the count of such columns.
All inputs are finite; a program needn't handle non-finite values.
Results may differ from the reference program's by a relative error of at most 0.0003.
Values sent between devices are 32-bit elements; how exact they have to be, the bound alone decides.
No kernel may reach another device: no remote copies, remote signals or barrier semaphores. Data moves between devices by JAX's collectives and lax.ppermute only.
A program may use at most 64 MiB of HBM per device.

```python
import math
import jax
import jax.numpy as jnp
from jax import lax

GRID = 16
PLY = 48
CASES = 2
SWEEPS = 3
STEPS = 2
SUB_DEV = 8
NODE_DEV = 8192
SUBS = 256
BOUNDARY = 64
ROWS = 512
MOST = 32
NODES = 262144
N_GRP = 4
N_SUB = 8


def coupling(key):
    devices = SUBS // SUB_DEV
    key_busy, key_rows, key_nodes = jax.random.split(jax.random.fold_in(key, 11), 3)
    busy_owner = jax.random.randint(key_busy, (), 0, devices)

    def block_owners(block_key):
        key_slots, key_order = jax.random.split(block_key)
        slots = jax.random.permutation(key_slots, devices * MOST)
        slot_owner = (slots // MOST).astype(jnp.int32)
        keep_order = jnp.argsort((slot_owner == busy_owner).astype(jnp.int32), stable=True)
        others = slot_owner[keep_order][:ROWS - MOST]
        chosen = jnp.concatenate([jnp.full((MOST,), busy_owner, jnp.int32), others])
        return chosen[jax.random.permutation(key_order, ROWS)]
    owners = jax.vmap(block_owners)(jax.random.split(key_rows, devices))
    local_node = jax.random.randint(key_nodes, (devices, ROWS), 0, NODE_DEV)
    owner_hit = (owners[:, :, None] == jnp.arange(devices)[None, None, :]).astype(jnp.int32)
    slot_rank = jnp.sum((jnp.cumsum(owner_hit, axis=1) - owner_hit) * owner_hit, axis=2)
    node_table = jnp.full((devices, devices, MOST), -1, jnp.int32)
    dest_block = jnp.broadcast_to(jnp.arange(devices)[:, None], (devices, ROWS))
    node_table = node_table.at[owners, dest_block, slot_rank].set(local_node)
    point_owner = owners.reshape(SUBS, BOUNDARY)
    return (point_owner, node_table)


def draw_point_owner(key, part):
    return coupling(key)[0]


def draw_owner_nodes(key, part):
    return coupling(key)[1]


def plant(array, own_key, low, largest):
    extent = array.shape
    spot = [jax.random.randint(jax.random.fold_in(own_key, axis), (), 0, extent[axis]) for axis in range(len(extent))]
    array = array.at[tuple(spot)].set(low)
    longest = extent.index(max(extent))
    spot[longest] = (spot[longest] + 1) % extent[longest]
    return array.at[tuple(spot)].set(largest)


def shard_levels(own_key, dims, cuts, least, largest):
    def one(position, parts):
        heights = jax.random.uniform(jax.random.fold_in(jax.random.fold_in(own_key, 6), position), (parts,), jnp.float32, least / len(cuts), largest / len(cuts))
        return jnp.repeat(jnp.exp(heights), dims[position] // parts).reshape((-1,) + (1,) * (len(dims) - position - 1))

    factor_of = one(*cuts[0])
    for cut in cuts[1:]:
        factor_of = factor_of * one(*cut)
    return factor_of


def scatter_about(key, extent, scale, limit, cuts=(), kind=jnp.bfloat16):
    result = scale * jax.random.normal(key, extent, jnp.float32)
    if cuts:
        result = result * shard_levels(key, extent, cuts, -0.22, 0.18)
    return jnp.clip(result, -limit, limit).astype(kind)


def setup_inputs(seed: int = 0) -> dict:
    keys = jax.random.split(jax.random.key(seed), 8)
    return {
        "shell_state": scatter_about(keys[0], (CASES, PLY, NODES), 1.0, 6.0, ((2, 32),), jnp.float32),
        "source": scatter_about(keys[1], (CASES, SUBS, GRID, PLY * GRID), 1.0, 6.0, ((1, 32),)),
        "knockdown": jnp.clip(jnp.exp(math.log(3.0) - 2.306499 * jax.random.uniform(keys[2], (SUBS, GRID, PLY * GRID), jnp.float32) ** shard_levels(keys[2], (SUBS, GRID, PLY * GRID), ((0, 32),), -0.2, 0.2)), 0.29882812, 3.0).astype(jnp.bfloat16),
        "orient": plant(jax.random.randint(keys[3], (SUBS, PLY), 0, 4), jax.random.fold_in(keys[3], 1), 0, 3).astype(jnp.int32),
        "active": plant(jax.random.randint(keys[4], (SUBS,), PLY // 2, PLY + 1), jax.random.fold_in(keys[4], 1), PLY // 2, PLY).astype(jnp.int32),
        "point_owner": draw_point_owner(jax.random.fold_in(keys[7], 71), 0),
        "owner_nodes": draw_owner_nodes(jax.random.fold_in(keys[7], 71), 0),
    }


FIBER_COND = 1.0
TRANSVERSE = 0.25
THROUGH = 0.15
MASS_SHARE = 0.05
CHEB_CENTER = 1.02
CHEB_HALF = 0.98


def face_mean(lower_side, upper_side):
    return jnp.where((lower_side > 0) & (upper_side > 0), 0.5 * (lower_side + upper_side), 0.0)


def cell_terms(knockdown, orient, active):
    ply_count = knockdown.shape[2]
    active_mask = (jnp.arange(ply_count)[None, :] < active[:, None]).astype(jnp.float32)
    ply_angle = orient.astype(jnp.float32) * (math.pi / 6.0)
    cos_square = jnp.cos(ply_angle) ** 2
    fiber_part = (FIBER_COND * cos_square + TRANSVERSE * (1.0 - cos_square)) * active_mask
    cross_part = (FIBER_COND * (1.0 - cos_square) + TRANSVERSE * cos_square) * active_mask
    along_x = knockdown * fiber_part[:, None, :, None]
    along_y = knockdown * cross_part[:, None, :, None]
    across_ply = knockdown * (THROUGH * active_mask)[:, None, :, None]
    return along_x, along_y, across_ply, active_mask[:, None, :, None]


def assemble(along_x, along_x_pad, along_y, across_ply, active_mask, x_position):
    side_cells = along_x.shape[3]
    face_west = face_mean(along_x_pad[:, :-2], along_x)
    face_east = face_mean(along_x, along_x_pad[:, 2:])
    edge_y = jnp.zeros(along_x.shape[:3] + (1,), along_x.dtype)
    inner_y = face_mean(along_y[..., :-1], along_y[..., 1:])
    face_south = jnp.concatenate([edge_y, inner_y], axis=3)
    face_north = jnp.concatenate([inner_y, edge_y], axis=3)
    edge_ply = jnp.zeros(along_x.shape[:2] + (1,) + along_x.shape[3:], along_x.dtype)
    inner_ply = face_mean(across_ply[:, :, :-1], across_ply[:, :, 1:])
    face_below = jnp.concatenate([edge_ply, inner_ply], axis=2)
    face_above = jnp.concatenate([inner_ply, edge_ply], axis=2)
    at_first = (x_position == 0)[None, :, None, None]
    at_final = (x_position == side_cells - 1)[None, :, None, None]
    column = jnp.arange(side_cells)
    ghost_west = jnp.where(at_first, along_x, 0.0)
    ghost_east = jnp.where(at_final, along_x, 0.0)
    ghost_south = jnp.where(column == 0, along_y, 0.0)
    ghost_north = jnp.where(column == side_cells - 1, along_y, 0.0)
    diagonal = (face_west + face_east + face_south + face_north + face_below + face_above
                + ghost_west + ghost_east + ghost_south + ghost_north
                + MASS_SHARE * (along_x + along_y + across_ply) + (1.0 - active_mask))
    return (face_west, face_east, face_south, face_north, face_below, face_above,
            ghost_west, ghost_east, ghost_south, ghost_north, diagonal)


def operate(field_in, field_pad, coeffs):
    face_west, face_east, face_south, face_north, face_below, face_above = coeffs[:6]
    diagonal = coeffs[10]
    zero_y = jnp.zeros(field_in.shape[:4] + (1,), field_in.dtype)
    zero_ply = jnp.zeros(field_in.shape[:3] + (1,) + field_in.shape[4:], field_in.dtype)
    from_south = jnp.concatenate([zero_y, field_in[..., :-1]], axis=4)
    from_north = jnp.concatenate([field_in[..., 1:], zero_y], axis=4)
    from_below = jnp.concatenate([zero_ply, field_in[:, :, :, :-1]], axis=3)
    from_above = jnp.concatenate([field_in[:, :, :, 1:], zero_ply], axis=3)
    beside = (face_west * field_pad[:, :, :-2] + face_east * field_pad[:, :, 2:]
              + face_south * from_south + face_north * from_north
              + face_below * from_below + face_above * from_above)
    return diagonal * field_in - beside


def pad_along_x(field_in):
    return jnp.pad(field_in, ((0, 0), (0, 0), (1, 1), (0, 0), (0, 0)))


def solve_cells(source, knockdown, orient, active, ghosts):
    case_count, sub_count, side_x, flat_width = source.shape
    ply_count = orient.shape[1]
    side_cells = flat_width // ply_count
    along_x, along_y, across_ply, active_mask = cell_terms(
        knockdown.astype(jnp.float32).reshape(sub_count, side_x, ply_count, side_cells), orient, active)
    along_x_pad = jnp.pad(along_x, ((0, 0), (1, 1), (0, 0), (0, 0)))
    coeffs = assemble(along_x, along_x_pad, along_y, across_ply, active_mask, jnp.arange(side_x))
    ghost_west, ghost_east, ghost_south, ghost_north, diagonal = coeffs[6:]
    value_west = ghosts[:, :, None, :, 0:side_cells]
    value_east = ghosts[:, :, None, :, side_cells:2 * side_cells]
    value_south = jnp.swapaxes(ghosts[:, :, :, 2 * side_cells:3 * side_cells], 2, 3)[..., None]
    value_north = jnp.swapaxes(ghosts[:, :, :, 3 * side_cells:], 2, 3)[..., None]
    field_cells = source.astype(jnp.float32).reshape(case_count, sub_count, side_x, ply_count, side_cells)
    residual = (active_mask * field_cells + ghost_west * value_west + ghost_east * value_east
                + ghost_south * value_south + ghost_north * value_north)
    adjoint = jnp.zeros_like(residual)
    sigma_ratio = CHEB_CENTER / CHEB_HALF
    for sweep_index in range(SWEEPS):
        rho_now = 1.0 / sigma_ratio
        direction = residual / (CHEB_CENTER * diagonal)
        for step_index in range(STEPS):
            adjoint = adjoint + direction
            if not (sweep_index + 1 == SWEEPS and step_index + 1 == STEPS):
                residual = residual - operate(direction, pad_along_x(direction), coeffs)
            if step_index + 1 < STEPS:
                rho_next = 1.0 / (2.0 * sigma_ratio - rho_now)
                direction = (rho_next * rho_now) * direction + (2.0 * rho_next / CHEB_HALF) * (residual / diagonal)
                rho_now = rho_next
    force_west = jnp.sum(ghost_west * (value_west - adjoint), axis=2)
    force_east = jnp.sum(ghost_east * (value_east - adjoint), axis=2)
    force_south = jnp.swapaxes(jnp.sum(ghost_south * (value_south - adjoint), axis=4), 2, 3)
    force_north = jnp.swapaxes(jnp.sum(ghost_north * (value_north - adjoint), axis=4), 2, 3)
    forces = jnp.concatenate([force_west, force_east, force_south, force_north], axis=3)
    return adjoint.reshape(case_count, sub_count, side_x, flat_width), forces


def point_nodes(point_owner, owner_nodes):
    devices = N_GRP * N_SUB
    blocks = point_owner.reshape(devices, ROWS)
    owner_hit = (blocks[:, :, None] == jnp.arange(devices)[None, None, :]).astype(jnp.int32)
    slot_rank = jnp.sum((jnp.cumsum(owner_hit, axis=1) - owner_hit) * owner_hit, axis=2)
    local_node = owner_nodes[blocks, jnp.arange(devices)[:, None], slot_rank]
    node_index = blocks * NODE_DEV + local_node
    return node_index.reshape(SUBS, BOUNDARY)


def reference(shell_state, source, knockdown, orient, active, point_owner, owner_nodes):
    node_index = point_nodes(point_owner, owner_nodes)
    ghosts = jnp.transpose(shell_state[:, :, node_index], (0, 2, 1, 3))

    def solve_one(sub_index):
        sub_source = lax.dynamic_slice_in_dim(source, sub_index, 1, 1)
        sub_knock = lax.dynamic_slice_in_dim(knockdown, sub_index, 1, 0)
        sub_orient = lax.dynamic_slice_in_dim(orient, sub_index, 1, 0)
        sub_active = lax.dynamic_slice_in_dim(active, sub_index, 1, 0)
        sub_ghosts = lax.dynamic_slice_in_dim(ghosts, sub_index, 1, 1)
        return solve_cells(sub_source, sub_knock, sub_orient, sub_active, sub_ghosts)

    adjoint, forces = lax.map(solve_one, jnp.arange(SUBS))
    adjoint = jnp.moveaxis(adjoint[:, :, 0], 0, 1)
    forces = jnp.transpose(forces[:, :, 0], (1, 2, 0, 3)).reshape(CASES, PLY, SUBS * BOUNDARY)
    shell_force = jnp.zeros((CASES, PLY, NODES), jnp.float32).at[:, :, node_index.reshape(-1)].add(forces)
    return adjoint, shell_force
```

```python
import functools
import math

import jax
import jax.numpy as jnp
from jax import lax
from jax.experimental import pallas as pl
from jax.experimental.pallas import tpu as pltpu
from jax.sharding import PartitionSpec as P

SWEEPS = 3
STEPS = 2

FIBER_COND = 1.0
TRANSVERSE = 0.25
THROUGH = 0.15
MASS_SHARE = 0.05
CHEB_CENTER = 1.02
CHEB_HALF = 0.98

LANES = 128
F32 = jnp.float32
BF16 = jnp.bfloat16


def packed_rows(slot_depth):
    return slot_depth * 3 // 4 if slot_depth % 32 == 0 else slot_depth


def pack_slots(rows_ref, out_ref, peers, slot_depth):
    if slot_depth % 32:
        out_ref[...] = rows_ref[...]
        return
    lane = lax.broadcasted_iota(jnp.int32, (8, LANES), 1)
    low = lane < 96
    for g in range(peers * slot_depth // 32):
        extra = rows_ref[g * 32 + 24 : g * 32 + 32, :]
        for k in range(3):
            shift = (96 - 32 * k) % LANES
            moved = pltpu.roll(extra, shift, 1)
            own = rows_ref[g * 32 + 8 * k : g * 32 + 8 * k + 8, :]
            out_ref[g * 24 + 8 * k : g * 24 + 8 * k + 8, :] = jnp.where(low, own, moved)


def unpack_slots(packed_ref, rows_ref, peers, slot_depth):
    if slot_depth % 32:
        rows_ref[...] = packed_ref[...]
        return
    lane = lax.broadcasted_iota(jnp.int32, (8, LANES), 1)
    for g in range(peers * slot_depth // 32):
        parts = []
        for k in range(3):
            own = packed_ref[g * 24 + 8 * k : g * 24 + 8 * k + 8, :]
            rows_ref[g * 32 + 8 * k : g * 32 + 8 * k + 8, :] = own
            parts.append(pltpu.roll(own, 32 + 32 * k, 1))
        extra = jnp.where(lane < 32, parts[0], jnp.where(lane < 64, parts[1], parts[2]))
        rows_ref[g * 32 + 24 : g * 32 + 32, :] = extra


def gather_kernel(node_ref, shell_ref, out_ref, turned, rows, *, peers, slot_depth):
    step = pl.program_id(0)
    chunk = shell_ref.shape[1]
    width = shell_ref.shape[0]
    for t in range(chunk // LANES):
        start = pl.multiple_of(step * chunk + t * LANES, LANES)
        turned[pl.ds(start, LANES), 0:width] = shell_ref[:, t * LANES : (t + 1) * LANES].T

    @pl.when(step == pl.num_programs(0) - 1)
    def _():
        def pick(group, carry):
            for u in range(16):
                slot = group * 16 + u
                node = jnp.maximum(node_ref[slot], 0)
                rows[pl.ds(slot, 1), :] = turned[pl.ds(node, 1), :]
            return carry

        lax.fori_loop(0, peers * slot_depth // 16, pick, 0)
        pack_slots(rows, out_ref, peers, slot_depth)


def gather_shell(shell_flat, nodes, peers, slot_depth):
    width, node_local = shell_flat.shape
    chunks = 8
    out_rows = peers * packed_rows(slot_depth)
    return pl.pallas_call(
        functools.partial(gather_kernel, peers=peers, slot_depth=slot_depth),
        out_shape=jax.ShapeDtypeStruct((out_rows, LANES), F32),
        grid_spec=pltpu.PrefetchScalarGridSpec(
            num_scalar_prefetch=1,
            grid=(chunks,),
            in_specs=[pl.BlockSpec((width, node_local // chunks), lambda i, n: (0, i))],
            out_specs=pl.BlockSpec((out_rows, LANES), lambda i, n: (0, 0)),
            scratch_shapes=[
                pltpu.VMEM((node_local, LANES), F32),
                pltpu.VMEM((peers * slot_depth, LANES), F32),
            ],
        ),
        compiler_params=pltpu.CompilerParams(vmem_limit_bytes=24 << 20),
        name="gather_shell",
    )(nodes, shell_flat)


def scatter_kernel(node_ref, packed_ref, out_ref, total, rows, *, peers, slot_depth):
    step = pl.program_id(0)
    chunk = out_ref.shape[1]
    width = out_ref.shape[0]
    node_local = total.shape[0] - 8

    @pl.when(step == 0)
    def _():
        unpack_slots(packed_ref, rows, peers, slot_depth)
        zero = jnp.zeros((64, LANES), F32)

        def clear(i, carry):
            total[pl.ds(pl.multiple_of(i * 64, 64), 64), :] = zero
            return carry

        lax.fori_loop(0, node_local // 64, clear, 0)
        total[node_local : node_local + 8, :] = jnp.zeros((8, LANES), F32)

        def put(group, carry):
            for u in range(8):
                slot = group * 8 + u
                node = node_ref[slot]
                node = jnp.where(node < 0, node_local, node)
                total[pl.ds(node, 1), :] += rows[pl.ds(slot, 1), :]
            return carry

        lax.fori_loop(0, peers * slot_depth // 8, put, 0)

    for t in range(chunk // LANES):
        start = pl.multiple_of(step * chunk + t * LANES, LANES)
        out_ref[:, t * LANES : (t + 1) * LANES] = total[pl.ds(start, LANES), 0:width].T


def scatter_forces(packed, nodes, peers, slot_depth, width, node_local):
    chunks = 8
    return pl.pallas_call(
        functools.partial(scatter_kernel, peers=peers, slot_depth=slot_depth),
        out_shape=jax.ShapeDtypeStruct((width, node_local), F32),
        grid_spec=pltpu.PrefetchScalarGridSpec(
            num_scalar_prefetch=1,
            grid=(chunks,),
            in_specs=[pl.BlockSpec(packed.shape, lambda i, n: (0, 0))],
            out_specs=pl.BlockSpec((width, node_local // chunks), lambda i, n: (0, i)),
            scratch_shapes=[
                pltpu.VMEM((node_local + 8, LANES), F32),
                pltpu.VMEM((peers * slot_depth, LANES), F32),
            ],
        ),
        compiler_params=pltpu.CompilerParams(vmem_limit_bytes=24 << 20),
        name="scatter_forces",
    )(nodes, packed)


def split_two(value):
    high = value.astype(BF16)
    return high, (value - high.astype(F32)).astype(BF16)


def solve_kernel(
    slot_ref, packed_ref, source_ref, knock_ref, ply_ref, spread_ref, spread_y_ref,
    fold_ref, fold_y_ref, adjoint_ref, out_ref,
    slots, bound, src, knock, face_x, face_y, face_p, diag, inverse, along_y, edge_x,
    work, resid, total, side_y, side_x, *, peers, slot_depth, plies, side,
):
    subs = 8
    cases = source_ref.shape[0]
    side_x_cells = source_ref.shape[2]
    width = source_ref.shape[3]
    tiles = width // LANES
    lane = lax.broadcasted_iota(jnp.int32, (subs, LANES), 1)
    y_place = lane % side
    first_y = y_place == 0
    last_y = y_place == side - 1
    low_ply = lane < side
    high_ply = lane >= LANES - side
    cut = [slice(t * LANES, (t + 1) * LANES) for t in range(tiles)]

    for s in range(subs):
        for t in range(tiles):
            knock[t, s * side_x_cells : (s + 1) * side_x_cells, :] = knock_ref[s, :, cut[t]].astype(F32)
            for c in range(cases):
                at = (c * subs + s) * side_x_cells
                src[t, at : at + side_x_cells, :] = source_ref[c, s, :, cut[t]].astype(F32)

    def plane(ref, x, base=0):
        return [ref[t, pl.ds(base + x, subs, stride=side_x_cells), :] for t in range(tiles)]

    def from_lower_ply(values):
        turned = [pltpu.roll(v, side, 1) for v in values]
        return [jnp.where(low_ply, turned[t - 1], turned[t]) for t in range(tiles)]

    def from_upper_ply(values):
        turned = [pltpu.roll(v, LANES - side, 1) for v in values]
        return [
            jnp.where(high_ply, turned[t + 1], turned[t]) for t in range(tiles - 1)
        ] + [turned[-1]]

    zero = jnp.zeros((subs, width), F32)
    face_x[0] = zero
    face_x[side_x_cells] = zero
    for k in range(2):
        for c in range(cases):
            work[k, c, 0] = zero
            work[k, c, side_x_cells + 1] = zero

    def faces_x(x, carry):
        here = plane(knock, x)
        there = plane(knock, x + 1)
        for t in range(tiles):
            fiber = ply_ref[0, :, cut[t]]
            face_x[x + 1, :, cut[t]] = 0.5 * (here[t] * fiber + there[t] * fiber)
        return carry

    lax.fori_loop(0, side_x_cells - 1, faces_x, 0)

    def coefficients(x, carry):
        k = plane(knock, x)
        ax = [k[t] * ply_ref[0, :, cut[t]] for t in range(tiles)]
        ay = [k[t] * ply_ref[1, :, cut[t]] for t in range(tiles)]
        ac = [k[t] * ply_ref[2, :, cut[t]] for t in range(tiles)]
        up = from_upper_ply(ac)
        fp = [ply_ref[4, :, cut[t]] * (ac[t] + up[t]) for t in range(tiles)]
        below = from_lower_ply(fp)
        at_edge = jnp.where((x == 0) | (x == side_x_cells - 1), 1.0, 0.0)
        for t in range(tiles):
            north = 0.5 * (ay[t] + pltpu.roll(ay[t], LANES - 1, 1))
            fy = jnp.where(last_y, 0.0, north)
            whole = (
                face_x[x, :, cut[t]]
                + face_x[x + 1, :, cut[t]]
                + pltpu.roll(fy, 1, 1)
                + fy
                + below[t]
                + fp[t]
                + at_edge * ax[t]
                + jnp.where(first_y | last_y, ay[t], 0.0)
                + MASS_SHARE * (ax[t] + ay[t] + ac[t])
                + (1.0 - ply_ref[3, :, cut[t]])
            )
            face_y[x, :, cut[t]] = fy
            face_p[x, :, cut[t]] = fp[t]
            diag[x, :, cut[t]] = whole
            inverse[x, :, cut[t]] = 1.0 / whole
            along_y[x, :, cut[t]] = ay[t]
        return carry

    lax.fori_loop(0, side_x_cells, coefficients, 0)
    for e, x in enumerate((0, side_x_cells - 1)):
        k = plane(knock, x)
        for t in range(tiles):
            edge_x[e, :, cut[t]] = k[t] * ply_ref[0, :, cut[t]]

    unpack_slots(packed_ref, slots, peers, slot_depth)
    points = 4 * side

    def fetch(q, carry):
        for s in range(subs):
            at = slot_ref[s * points + q]
            bound[pl.ds(q * subs + s, 1), :] = slots[pl.ds(at, 1), :]
        return carry

    lax.fori_loop(0, points, fetch, 0, unroll=4)

    rows = side * subs
    for c in range(cases):
        for e in range(2):
            high, low = split_two(bound[e * rows : (e + 1) * rows, :])
            spread = jnp.dot(
                jnp.concatenate([high, low], axis=1), spread_ref[c], preferred_element_type=F32
            )
            for t in range(tiles):
                gathered = jnp.zeros((subs, LANES), F32)
                for q in range(side):
                    part = spread[q * subs : (q + 1) * subs, cut[t]]
                    gathered = jnp.where(y_place == q, part, gathered)
                side_x[c, e, :, cut[t]] = gathered
        pieces = []
        for e in range(2, 4):
            pieces += split_two(bound[e * rows : (e + 1) * rows, :])
        side_y[c] = jnp.dot(
            jnp.concatenate(pieces, axis=1), spread_y_ref[c], preferred_element_type=F32
        )

    def residual(x, carry):
        at_first = jnp.where(x == 0, 1.0, 0.0)
        at_final = jnp.where(x == side_x_cells - 1, 1.0, 0.0)
        row = pl.multiple_of(x * subs, subs)
        for c in range(cases):
            field = plane(src, x, c * subs * side_x_cells)
            for t in range(tiles):
                value = (
                    ply_ref[3, :, cut[t]] * field[t]
                    + along_y[x, :, cut[t]] * side_y[c, pl.ds(row, subs), cut[t]]
                    + at_first * (edge_x[0, :, cut[t]] * side_x[c, 0, :, cut[t]])
                    + at_final * (edge_x[1, :, cut[t]] * side_x[c, 1, :, cut[t]])
                )
                resid[c, x, :, cut[t]] = value
                work[0, c, x + 1, :, cut[t]] = (value * inverse[x, :, cut[t]]) * (1.0 / CHEB_CENTER)
        return carry

    lax.fori_loop(0, side_x_cells, residual, 0)

    def operate(x, c, old):
        w = [work[old, c, x + 1, :, cut[t]] for t in range(tiles)]
        fp = [face_p[x, :, cut[t]] for t in range(tiles)]
        below = from_lower_ply([fp[t] * w[t] for t in range(tiles)])
        above = from_upper_ply(w)
        out = []
        for t in range(tiles):
            fy = face_y[x, :, cut[t]]
            beside = (
                face_x[x, :, cut[t]] * work[old, c, x, :, cut[t]]
                + face_x[x + 1, :, cut[t]] * work[old, c, x + 2, :, cut[t]]
                + pltpu.roll(fy * w[t], 1, 1)
                + fy * pltpu.roll(w[t], LANES - 1, 1)
                + (below[t] + fp[t] * above[t])
            )
            out.append(diag[x, :, cut[t]] * w[t] - beside)
        return w, out

    sigma = CHEB_CENTER / CHEB_HALF
    rho_first = 1.0 / sigma
    rho_next = 1.0 / (2.0 * sigma - rho_first)
    keep = rho_next * rho_first
    gain = 2.0 * rho_next / CHEB_HALF

    for sweep in range(SWEEPS):
        final = sweep == SWEEPS - 1

        def second(x, carry, sweep=sweep, final=final):
            for c in range(cases):
                w, moved = operate(x, c, 0)
                for t in range(tiles):
                    r = resid[c, x, :, cut[t]] - moved[t]
                    later = keep * w[t] + gain * (r * inverse[x, :, cut[t]])
                    sums = w[t] + later
                    if sweep:
                        sums = total[c, x, :, cut[t]] + sums
                    total[c, x, :, cut[t]] = sums
                    if not final:
                        resid[c, x, :, cut[t]] = r
                        work[1, c, x + 1, :, cut[t]] = later
            return carry

        lax.fori_loop(0, side_x_cells, second, 0)
        if final:
            break

        def first(x, carry):
            for c in range(cases):
                _, moved = operate(x, c, 1)
                for t in range(tiles):
                    r = resid[c, x, :, cut[t]] - moved[t]
                    resid[c, x, :, cut[t]] = r
                    work[0, c, x + 1, :, cut[t]] = (r * inverse[x, :, cut[t]]) * (1.0 / CHEB_CENTER)
            return carry

        lax.fori_loop(0, side_x_cells, first, 0)

    def force_y(x, carry):
        row = pl.multiple_of(x * subs, subs)
        for c in range(cases):
            for t in range(tiles):
                value = total[c, x, :, cut[t]]
                src[t, pl.ds(c * subs * side_x_cells + x, subs, stride=side_x_cells), :] = value
                side_y[c, pl.ds(row, subs), cut[t]] = along_y[x, :, cut[t]] * (
                    side_y[c, pl.ds(row, subs), cut[t]] - value
                )
        return carry

    lax.fori_loop(0, side_x_cells, force_y, 0)
    for t in range(tiles):
        adjoint_ref[:, cut[t]] = src[t]

    sums_x = [jnp.zeros((rows, LANES), F32) for _ in range(2)]
    sums_y = jnp.zeros((rows, 2 * LANES), F32)
    for c in range(cases):
        for piece in split_two(side_y[c]):
            sums_y = sums_y + jnp.dot(piece, fold_y_ref[c], preferred_element_type=F32)
        for e, x in enumerate((0, side_x_cells - 1)):
            at_ply = edge_x[e] * (side_x[c, e] - total[c, x])
            y_wide = lax.broadcasted_iota(jnp.int32, (subs, width), 1) % side
            for piece in split_two(at_ply):
                wide = piece.astype(F32)
                tall = jnp.concatenate(
                    [jnp.where(y_wide == q, wide, 0.0) for q in range(side)], axis=0
                ).astype(BF16)
                sums_x[e] = sums_x[e] + jnp.dot(tall, fold_ref[c], preferred_element_type=F32)
    bound[0:rows, :] = sums_x[0]
    bound[rows : 2 * rows, :] = sums_x[1]
    bound[2 * rows : 3 * rows, :] = sums_y[:, :LANES]
    bound[3 * rows : 4 * rows, :] = sums_y[:, LANES:]

    def post(q, carry):
        for s in range(subs):
            at = slot_ref[s * points + q]
            slots[pl.ds(at, 1), :] = bound[pl.ds(q * subs + s, 1), :]
        return carry

    lax.fori_loop(0, points, post, 0, unroll=4)
    pack_slots(slots, out_ref, peers, slot_depth)


def solve_block(packed, slot_index, source, knockdown, ply_terms, tables, peers, slot_depth):
    cases, subs, side_x, width = source.shape
    plies = width // side_x
    side = width // plies
    vm = pl.BlockSpec(memory_space=pltpu.VMEM)
    out_rows = peers * packed_rows(slot_depth)
    planes = (side_x, subs, width)
    scratch = [
        pltpu.VMEM((peers * slot_depth, LANES), F32),
        pltpu.VMEM((4 * side * subs, LANES), F32),
        pltpu.VMEM((width // LANES, cases * subs * side_x, LANES), F32),
        pltpu.VMEM((width // LANES, subs * side_x, LANES), F32),
        pltpu.VMEM((side_x + 1, subs, width), F32),
        pltpu.VMEM(planes, F32),
        pltpu.VMEM(planes, F32),
        pltpu.VMEM(planes, F32),
        pltpu.VMEM(planes, F32),
        pltpu.VMEM(planes, F32),
        pltpu.VMEM((2, subs, width), F32),
        pltpu.VMEM((2, cases, side_x + 2, subs, width), F32),
        pltpu.VMEM((cases,) + planes, F32),
        pltpu.VMEM((cases,) + planes, F32),
        pltpu.VMEM((cases, side_x * subs, width), F32),
        pltpu.VMEM((cases, 2, subs, width), F32),
    ]
    adjoint, outbound = pl.pallas_call(
        functools.partial(
            solve_kernel, peers=peers, slot_depth=slot_depth, plies=plies, side=side
        ),
        out_shape=(
            jax.ShapeDtypeStruct((cases * subs * side_x, width), F32),
            jax.ShapeDtypeStruct((out_rows, LANES), F32),
        ),
        in_specs=[pl.BlockSpec(memory_space=pltpu.SMEM)] + [vm] * 8,
        out_specs=(vm, vm),
        scratch_shapes=scratch,
        compiler_params=pltpu.CompilerParams(vmem_limit_bytes=32 << 20),
        name="solve_block",
    )(slot_index, packed, source, knockdown, ply_terms, *tables)
    return adjoint.reshape(source.shape), outbound


def ply_table(orient, active, side):
    plies = orient.shape[1]
    index = jnp.arange(plies)[None, :]
    mask = (index < active[:, None]).astype(F32)
    upper = ((index + 1 < active[:, None]) & (index + 1 < plies)).astype(F32)
    cos_square = jnp.cos(orient.astype(F32) * (math.pi / 6.0)) ** 2
    fiber = (FIBER_COND * cos_square + TRANSVERSE * (1.0 - cos_square)) * mask
    cross = (FIBER_COND * (1.0 - cos_square) + TRANSVERSE * cos_square) * mask
    terms = jnp.stack([fiber, cross, THROUGH * mask, mask, 0.5 * upper])
    return jnp.repeat(terms, side, axis=2)


def spread_tables(cases, plies, side):
    width = plies * side
    lane = jnp.arange(LANES)[:, None]
    cell = jnp.arange(width)[None, :]
    spread, spread_y, fold, fold_y = [], [], [], []
    for c in range(cases):
        hit = lane == c * plies + cell // side
        at_south = hit & (cell % side == 0)
        at_north = hit & (cell % side == side - 1)
        spread.append(jnp.concatenate([hit, hit], axis=0))
        spread_y.append(jnp.concatenate([at_south, at_south, at_north, at_north], axis=0))
        fold.append(hit.T)
        fold_y.append(jnp.concatenate([at_south.T, at_north.T], axis=1))
    return [jnp.stack(m).astype(BF16) for m in (spread, spread_y, fold, fold_y)]


def per_device(shell_state, source, knockdown, orient, active, point_owner, owner_nodes):
    cases, subs, side_x, width = source.shape
    plies = orient.shape[1]
    side = width // plies
    node_local = shell_state.shape[2]
    peers = owner_nodes.shape[1]
    slot_depth = owner_nodes.shape[2]
    axes = ("grp", "sub")
    per_peer = packed_rows(slot_depth)

    nodes = owner_nodes.reshape(peers * slot_depth)
    picked = gather_shell(
        shell_state.reshape(cases * plies, node_local), nodes, peers, slot_depth
    )
    arrived = lax.all_to_all(
        picked.reshape(peers, per_peer, LANES), axes, split_axis=0, concat_axis=0, tiled=True
    )

    owners = point_owner.reshape(-1)
    place = jnp.arange(owners.shape[0])
    earlier = (owners[:, None] == owners[None, :]) & (place[None, :] < place[:, None])
    slot_index = owners * slot_depth + jnp.sum(earlier.astype(jnp.int32), axis=1)

    adjoint, outbound = solve_block(
        arrived.reshape(peers * per_peer, LANES), slot_index, source, knockdown,
        ply_table(orient, active, side), spread_tables(cases, plies, side), peers, slot_depth,
    )
    returned = lax.all_to_all(
        outbound.reshape(peers, per_peer, LANES), axes, split_axis=0, concat_axis=0, tiled=True
    )
    force = scatter_forces(
        returned.reshape(peers * per_peer, LANES), nodes, peers, slot_depth,
        cases * plies, node_local,
    )
    return adjoint, force.reshape(cases, plies, node_local)


def solution(mesh):
    in_specs = (
        P(None, None, ("grp", "sub")),
        P(None, ("grp", "sub"), None, None),
        P(("grp", "sub"), None, None),
        P(("grp", "sub"), None),
        P(("grp", "sub")),
        P(("grp", "sub"), None),
        P(("grp", "sub"), None, None),
    )
    out_specs = (P(None, ("grp", "sub"), None, None), P(None, None, ("grp", "sub")))
    return jax.shard_map(
        per_device, mesh=mesh, in_specs=in_specs, out_specs=out_specs, check_vma=False
    )
```

```python
import functools
import math

import jax
import jax.numpy as jnp
from jax import lax
from jax.experimental import pallas as pl
from jax.experimental.pallas import tpu as pltpu
from jax.sharding import PartitionSpec as P

SWEEPS = 3
STEPS = 2

FIBER_COND = 1.0
TRANSVERSE = 0.25
THROUGH = 0.15
MASS_SHARE = 0.05
CHEB_CENTER = 1.02
CHEB_HALF = 0.98

LANES = 128
HALF = 64
F32 = jnp.float32
BF16 = jnp.bfloat16


def packed_rows(slot_depth):
    return slot_depth * 3 // 4 if slot_depth % 32 == 0 else slot_depth


def pack_slots(rows_ref, out_ref, peers, slot_depth):
    used = lax.broadcasted_iota(jnp.int32, (8, LANES), 1) % HALF < 48
    if slot_depth % 32:
        for g in range(peers * slot_depth // 8):
            part = slice(g * 8, g * 8 + 8)
            out_ref[part, :] = jnp.where(used, rows_ref[part, :], 0.0)
        return
    for g in range(peers * slot_depth // 32):
        extra = rows_ref[g * 32 + 24 : g * 32 + 32, :]
        for k in range(3):
            moved = pltpu.roll(extra, 48 - 16 * k, 1)
            own = rows_ref[g * 32 + 8 * k : g * 32 + 8 * k + 8, :]
            out_ref[g * 24 + 8 * k : g * 24 + 8 * k + 8, :] = jnp.where(used, own, moved)


def unpack_slots(packed_ref, rows_ref, peers, slot_depth):
    if slot_depth % 32:
        rows_ref[...] = packed_ref[...]
        return
    third = lax.broadcasted_iota(jnp.int32, (8, LANES), 1) % HALF // 16
    for g in range(peers * slot_depth // 32):
        parts = []
        for k in range(3):
            own = packed_ref[g * 24 + 8 * k : g * 24 + 8 * k + 8, :]
            rows_ref[g * 32 + 8 * k : g * 32 + 8 * k + 8, :] = own
            parts.append(pltpu.roll(own, LANES - 48 + 16 * k, 1))
        extra = jnp.where(third == 0, parts[0], jnp.where(third == 1, parts[1], parts[2]))
        rows_ref[g * 32 + 24 : g * 32 + 32, :] = extra


def gather_kernel(node_ref, shell_hbm, out_ref, shell, turned, rows, sems, *, peers, slot_depth):
    width, node_local = shell.shape
    chunks = sems.shape[0]
    chunk = node_local // chunks
    copies = []
    for i in range(chunks):
        part = slice(i * chunk, (i + 1) * chunk)
        copies.append(pltpu.make_async_copy(shell_hbm.at[:, part], shell.at[:, part], sems.at[i]))
        copies[i].start()
    gap = jnp.zeros((HALF - width // 2, LANES), F32)
    for i in range(chunks):
        copies[i].wait()
        for t in range(i * chunk // LANES, (i + 1) * chunk // LANES):
            tile = shell[:, t * LANES : (t + 1) * LANES]
            parts = [tile[: width // 2], gap, tile[width // 2 :], gap]
            turned[8 + t * LANES : 8 + (t + 1) * LANES, :] = jnp.concatenate(parts, axis=0).T
    turned[0:8, :] = turned[8:16, :]

    def pick(peer, carry):
        for u in range(slot_depth):
            slot = peer * slot_depth + u
            rows[pl.ds(slot, 1), :] = turned[pl.ds(node_ref[peer, u] + 8, 1), :]
        return carry

    lax.fori_loop(0, peers, pick, 0)
    pack_slots(rows, out_ref, peers, slot_depth)


def gather_shell(shell_flat, nodes):
    width, node_local = shell_flat.shape
    peers, slot_depth = nodes.shape
    chunks = 8
    out_rows = peers * packed_rows(slot_depth)
    return pl.pallas_call(
        functools.partial(gather_kernel, peers=peers, slot_depth=slot_depth),
        out_shape=jax.ShapeDtypeStruct((out_rows, LANES), F32),
        in_specs=[
            pl.BlockSpec(memory_space=pltpu.SMEM),
            pl.BlockSpec(memory_space=pltpu.HBM),
        ],
        out_specs=pl.BlockSpec(memory_space=pltpu.VMEM),
        scratch_shapes=[
            pltpu.VMEM((width, node_local), F32),
            pltpu.VMEM((node_local + 8, LANES), F32),
            pltpu.VMEM((peers * slot_depth, LANES), F32),
            pltpu.SemaphoreType.DMA((chunks,)),
        ],
        name="gather_shell",
    )(nodes, shell_flat)


def scatter_kernel(node_ref, packed_ref, out_hbm, total, rows, out, sems, *, peers, slot_depth):
    width, node_local = out.shape
    unpack_slots(packed_ref, rows, peers, slot_depth)
    zero = jnp.zeros((64, LANES), F32)
    total[0:8, :] = jnp.zeros((8, LANES), F32)

    def clear(i, carry):
        total[pl.ds(pl.multiple_of(8 + i * 64, 8), 64), :] = zero
        return carry

    lax.fori_loop(0, node_local // 64, clear, 0)

    def put(peer, carry):
        for u in range(slot_depth):
            slot = peer * slot_depth + u
            total[pl.ds(node_ref[peer, u] + 8, 1), :] += rows[pl.ds(slot, 1), :]
        return carry

    lax.fori_loop(0, peers, put, 0)

    chunks = sems.shape[0]
    chunk = node_local // chunks
    copies = []
    for i in range(chunks):
        for t in range(i * chunk // LANES, (i + 1) * chunk // LANES):
            tile = total[8 + t * LANES : 8 + (t + 1) * LANES, :].T
            out[: width // 2, t * LANES : (t + 1) * LANES] = tile[: width // 2]
            out[width // 2 :, t * LANES : (t + 1) * LANES] = tile[HALF : HALF + width // 2]
        part = slice(i * chunk, (i + 1) * chunk)
        copies.append(pltpu.make_async_copy(out.at[:, part], out_hbm.at[:, part], sems.at[i]))
        copies[i].start()
    for i in range(chunks):
        copies[i].wait()


def scatter_forces(packed, nodes, width, node_local):
    peers, slot_depth = nodes.shape
    chunks = 8
    return pl.pallas_call(
        functools.partial(scatter_kernel, peers=peers, slot_depth=slot_depth),
        out_shape=jax.ShapeDtypeStruct((width, node_local), F32),
        in_specs=[
            pl.BlockSpec(memory_space=pltpu.SMEM),
            pl.BlockSpec(memory_space=pltpu.VMEM),
        ],
        out_specs=pl.BlockSpec(memory_space=pltpu.HBM),
        scratch_shapes=[
            pltpu.VMEM((node_local + 8, LANES), F32),
            pltpu.VMEM((peers * slot_depth, LANES), F32),
            pltpu.VMEM((width, node_local), F32),
            pltpu.SemaphoreType.DMA((chunks,)),
        ],
        name="scatter_forces",
    )(nodes, packed)


def split_two(value):
    high = value.astype(BF16)
    return high, (value - high.astype(F32)).astype(BF16)


def from_lower_ply(values, low_ply, side):
    turned = [pltpu.roll(v, side, 1) for v in values]
    return [jnp.where(low_ply, turned[t - 1], turned[t]) for t in range(len(values))]


def from_upper_ply(values, high_ply, side):
    turned = [pltpu.roll(v, LANES - side, 1) for v in values]
    return [
        jnp.where(high_ply, turned[t + 1], turned[t]) for t in range(len(values) - 1)
    ] + [turned[-1]]


def prepare_kernel(
    source_ref, knock_ref, cosine_ref, active_ref, slot_col_ref, slot_row_ref,
    planes_hbm, field_hbm, turned_hit_hbm, edge_x, hit_ref, spread_ref, fold_ref, fold_y_ref,
    planes, field, turned_hit_ref, src, knock, ply_ref, sems, *, plies, side,
):
    cases, subs, cells_x, width = source_ref.shape
    tiles = width // LANES
    lane = lax.broadcasted_iota(jnp.int32, (subs, LANES), 1)
    y_place = lane % side
    first_y = y_place == 0
    last_y = y_place == side - 1
    low_ply = lane < side
    high_ply = lane >= LANES - side
    cut = [slice(t * LANES, (t + 1) * LANES) for t in range(tiles)]

    def indicator(condition):
        return jnp.where(condition, 1.0, 0.0).astype(BF16)

    tall = spread_ref.shape[1]
    row = lax.broadcasted_iota(jnp.int32, (tall, width), 0) % LANES - HALF
    cell = lax.broadcasted_iota(jnp.int32, (tall, width), 1)
    own = row == cell // side
    y_cell = cell % side
    spread_ref[0] = indicator(own)
    spread_ref[1] = indicator(own & (y_cell == 0))
    spread_ref[2] = indicator(own & (y_cell == side - 1))
    cell = lax.broadcasted_iota(jnp.int32, (width, LANES), 0)
    own = lax.broadcasted_iota(jnp.int32, (width, LANES), 1) == cell // side
    y_cell = cell % side
    fold_ref[...] = indicator(own)
    fold_y_ref[:, :LANES] = indicator(own & (y_cell == 0))
    fold_y_ref[:, LANES:] = indicator(own & (y_cell == side - 1))

    rows, slots = hit_ref.shape
    hit_ref[...] = indicator(
        lax.broadcasted_iota(jnp.int32, (rows, slots), 1) == slot_col_ref[...]
    )
    turned_hit_ref[...] = indicator(
        lax.broadcasted_iota(jnp.int32, (slots, rows), 0) == slot_row_ref[...]
    )
    turned_copy = pltpu.make_async_copy(turned_hit_ref, turned_hit_hbm, sems.at[0])
    turned_copy.start()

    ply = lax.broadcasted_iota(jnp.int32, (subs, LANES), 1)
    mask = jnp.where(ply < active_ref[...], 1.0, 0.0)
    upper = jnp.where((ply + 1 < active_ref[...]) & (ply + 1 < plies), 0.5, 0.0)
    cos_square = cosine_ref[...]
    terms = jnp.concatenate(
        [
            (FIBER_COND * cos_square + TRANSVERSE * (1.0 - cos_square)) * mask,
            (FIBER_COND * (1.0 - cos_square) + TRANSVERSE * cos_square) * mask,
            mask,
            upper,
        ],
        axis=0,
    )
    high, low = split_two(terms)
    only = spread_ref[0, HALF : HALF + LANES, :]
    spread_terms = jnp.dot(high, only, preferred_element_type=F32) + jnp.dot(
        low, only, preferred_element_type=F32
    )
    for k in range(4):
        ply_ref[k] = spread_terms[k * subs : (k + 1) * subs, :]

    for s in range(subs):
        for t in range(tiles):
            knock[t, s * cells_x : (s + 1) * cells_x, :] = knock_ref[s, :, cut[t]].astype(F32)
            for c in range(cases):
                at = (c * subs + s) * cells_x
                src[t, at : at + cells_x, :] = source_ref[c, s, :, cut[t]].astype(F32)

    def plane(ref, x, base=0):
        return [ref[t, pl.ds(base + x, subs, stride=cells_x), :] for t in range(tiles)]

    face_x, face_y, face_p, diag, inverse, along_y = (planes.at[k] for k in range(6))
    face_x[0] = jnp.zeros((subs, width), F32)
    face_x[cells_x] = jnp.zeros((subs, width), F32)

    def faces_x(x, carry):
        here = plane(knock, x)
        there = plane(knock, x + 1)
        for t in range(tiles):
            fiber = ply_ref[0, :, cut[t]]
            face_x[x + 1, :, cut[t]] = 0.5 * (here[t] * fiber + there[t] * fiber)
        return carry

    lax.fori_loop(0, cells_x - 1, faces_x, 0)

    def coefficients(x, carry):
        k = plane(knock, x)
        ax = [k[t] * ply_ref[0, :, cut[t]] for t in range(tiles)]
        ay = [k[t] * ply_ref[1, :, cut[t]] for t in range(tiles)]
        ac = [k[t] * (THROUGH * ply_ref[2, :, cut[t]]) for t in range(tiles)]
        up = from_upper_ply(ac, high_ply, side)
        fp = [ply_ref[3, :, cut[t]] * (ac[t] + up[t]) for t in range(tiles)]
        below = from_lower_ply(fp, low_ply, side)
        at_edge = jnp.where((x == 0) | (x == cells_x - 1), 1.0, 0.0)
        for t in range(tiles):
            fy = jnp.where(last_y, 0.0, 0.5 * (ay[t] + pltpu.roll(ay[t], LANES - 1, 1)))
            whole = (
                face_x[x, :, cut[t]]
                + face_x[x + 1, :, cut[t]]
                + pltpu.roll(fy, 1, 1)
                + fy
                + below[t]
                + fp[t]
                + at_edge * ax[t]
                + jnp.where(first_y | last_y, ay[t], 0.0)
                + MASS_SHARE * (ax[t] + ay[t] + ac[t])
                + (1.0 - ply_ref[2, :, cut[t]])
            )
            face_y[x, :, cut[t]] = fy
            face_p[x, :, cut[t]] = fp[t]
            diag[x, :, cut[t]] = whole
            inverse[x, :, cut[t]] = 1.0 / whole
            along_y[x, :, cut[t]] = ay[t]
            for c in range(cases):
                value = src[t, pl.ds(c * subs * cells_x + x, subs, stride=cells_x), :]
                field[c, x, :, cut[t]] = ply_ref[2, :, cut[t]] * value
        return carry

    lax.fori_loop(0, cells_x, coefficients, 0)
    copies = [
        pltpu.make_async_copy(planes, planes_hbm, sems.at[1]),
        pltpu.make_async_copy(field, field_hbm, sems.at[2]),
    ]
    for copy in copies:
        copy.start()
    for e, x in enumerate((0, cells_x - 1)):
        k = plane(knock, x)
        for t in range(tiles):
            edge_x[e, :, cut[t]] = k[t] * ply_ref[0, :, cut[t]]
    for copy in [turned_copy] + copies:
        copy.wait()


def prepare(source, knockdown, orient, active, slot_index, slots):
    cases, subs, cells_x, width = source.shape
    plies = orient.shape[1]
    side = width // plies
    rows = slot_index.shape[0]
    cosine = jnp.cos(orient.astype(F32) * (math.pi / 6.0)) ** 2
    cosine = jnp.pad(cosine, ((0, 0), (0, LANES - plies)))
    slot_turned = slot_index.reshape(subs, rows // subs).T.reshape(rows)
    planes = (6, cells_x + 1, subs, width)
    field = (cases, cells_x, subs, width)
    vm = pl.BlockSpec(memory_space=pltpu.VMEM)
    hbm = pl.BlockSpec(memory_space=pltpu.HBM)
    shapes = [
        (planes, F32),
        (field, F32),
        ((slots, rows), BF16),
        ((2, subs, width), F32),
        ((rows, slots), BF16),
        ((3, 2 * LANES + HALF, width), BF16),
        ((width, LANES), BF16),
        ((width, 2 * LANES), BF16),
    ]
    return pl.pallas_call(
        functools.partial(prepare_kernel, plies=plies, side=side),
        out_shape=[jax.ShapeDtypeStruct(*shape) for shape in shapes],
        in_specs=[vm] * 6,
        out_specs=[hbm] * 3 + [vm] * 5,
        scratch_shapes=[
            pltpu.VMEM(planes, F32),
            pltpu.VMEM(field, F32),
            pltpu.VMEM((slots, rows), BF16),
            pltpu.VMEM((width // LANES, cases * subs * cells_x, LANES), F32),
            pltpu.VMEM((width // LANES, subs * cells_x, LANES), F32),
            pltpu.VMEM((4, subs, width), F32),
            pltpu.SemaphoreType.DMA((3,)),
        ],
        cost_estimate=pl.CostEstimate(
            flops=40_000_000, bytes_accessed=12_000_000, transcendentals=0
        ),
        name="prepare",
    )(source, knockdown, cosine, active[:, None], slot_turned[:, None], slot_turned[None, :])


def solve_kernel(
    packed_ref, planes_hbm, field_hbm, turned_hit_hbm, edge_x, hit_ref, spread_ref, fold_ref,
    fold_y_ref, total_hbm, out_ref,
    planes, field, turned_hit_ref, total, slots, bound, work, resid, side_y, side_x, sems,
    *, peers, slot_depth, side,
):
    copies = [
        pltpu.make_async_copy(field_hbm, field, sems.at[0]),
        pltpu.make_async_copy(planes_hbm, planes, sems.at[1]),
        pltpu.make_async_copy(turned_hit_hbm, turned_hit_ref, sems.at[2]),
    ]
    for copy in copies:
        copy.start()
    face_x, face_y, face_p, diag, inverse, along_y = (planes.at[k] for k in range(6))
    cases, cells_x, subs, width = field.shape
    tiles = width // LANES
    lane = lax.broadcasted_iota(jnp.int32, (subs, LANES), 1)
    y_place = lane % side
    low_ply = lane < side
    high_ply = lane >= LANES - side
    cut = [slice(t * LANES, (t + 1) * LANES) for t in range(tiles)]

    zero = jnp.zeros((subs, width), F32)
    for k in range(2):
        for c in range(cases):
            work[k, c, 0] = zero
            work[k, c, cells_x + 1] = zero

    unpack_slots(packed_ref, slots, peers, slot_depth)
    pieces = jnp.concatenate(split_two(slots[...]), axis=1)
    bound[...] = jnp.dot(hit_ref[...], pieces, preferred_element_type=F32).astype(BF16)

    rows = side * subs
    for c in range(cases):
        own = slice((1 - c) * HALF, (1 - c) * HALF + 2 * LANES)
        for e in range(2):
            spread = jnp.dot(
                bound[e * rows : (e + 1) * rows, :],
                spread_ref[0, own, :],
                preferred_element_type=F32,
            )
            for t in range(tiles):
                gathered = spread[0:subs, cut[t]]
                for q in range(1, side):
                    part = spread[q * subs : (q + 1) * subs, cut[t]]
                    gathered = jnp.where(y_place == q, part, gathered)
                side_x[c, e, :, cut[t]] = gathered
        side_y[c] = jnp.dot(
            bound[2 * rows : 3 * rows, :], spread_ref[1, own, :], preferred_element_type=F32
        ) + jnp.dot(
            bound[3 * rows : 4 * rows, :], spread_ref[2, own, :], preferred_element_type=F32
        )
    for copy in copies[:2]:
        copy.wait()

    def residual(x, carry):
        at_first = jnp.where(x == 0, 1.0, 0.0)
        at_final = jnp.where(x == cells_x - 1, 1.0, 0.0)
        row = pl.multiple_of(x * subs, subs)
        for c in range(cases):
            for t in range(tiles):
                value = (
                    field[c, x, :, cut[t]]
                    + along_y[x, :, cut[t]] * side_y[c, pl.ds(row, subs), cut[t]]
                    + at_first * (edge_x[0, :, cut[t]] * side_x[c, 0, :, cut[t]])
                    + at_final * (edge_x[1, :, cut[t]] * side_x[c, 1, :, cut[t]])
                )
                resid[c, x, :, cut[t]] = value
                work[0, c, x + 1, :, cut[t]] = (value * inverse[x, :, cut[t]]) * (1.0 / CHEB_CENTER)
        return carry

    lax.fori_loop(0, cells_x, residual, 0, unroll=4)

    def operate(x, c, old):
        w = [work[old, c, x + 1, :, cut[t]] for t in range(tiles)]
        fp = [face_p[x, :, cut[t]] for t in range(tiles)]
        below = from_lower_ply([fp[t] * w[t] for t in range(tiles)], low_ply, side)
        above = from_upper_ply(w, high_ply, side)
        out = []
        for t in range(tiles):
            fy = face_y[x, :, cut[t]]
            beside = (
                face_x[x, :, cut[t]] * work[old, c, x, :, cut[t]]
                + face_x[x + 1, :, cut[t]] * work[old, c, x + 2, :, cut[t]]
                + pltpu.roll(fy * w[t], 1, 1)
                + fy * pltpu.roll(w[t], LANES - 1, 1)
                + (below[t] + fp[t] * above[t])
            )
            out.append(diag[x, :, cut[t]] * w[t] - beside)
        return w, out

    sigma = CHEB_CENTER / CHEB_HALF
    rho_first = 1.0 / sigma
    rho_next = 1.0 / (2.0 * sigma - rho_first)
    keep = rho_next * rho_first
    gain = 2.0 * rho_next / CHEB_HALF

    for sweep in range(SWEEPS):
        final = sweep == SWEEPS - 1

        def second(x, carry, sweep=sweep, final=final):
            for c in range(cases):
                w, moved = operate(x, c, 0)
                for t in range(tiles):
                    r = resid[c, x, :, cut[t]] - moved[t]
                    later = keep * w[t] + gain * (r * inverse[x, :, cut[t]])
                    sums = w[t] + later
                    if sweep:
                        sums = total[c, x, :, cut[t]] + sums
                    total[c, x, :, cut[t]] = sums
                    if not final:
                        resid[c, x, :, cut[t]] = r
                        work[1, c, x + 1, :, cut[t]] = later
                    else:
                        row = pl.multiple_of(x * subs, subs)
                        side_y[c, pl.ds(row, subs), cut[t]] = along_y[x, :, cut[t]] * (
                            side_y[c, pl.ds(row, subs), cut[t]] - sums
                        )
            return carry

        lax.fori_loop(0, cells_x, second, 0, unroll=True)
        if final:
            break

        def first(x, carry):
            for c in range(cases):
                _, moved = operate(x, c, 1)
                for t in range(tiles):
                    r = resid[c, x, :, cut[t]] - moved[t]
                    resid[c, x, :, cut[t]] = r
                    work[0, c, x + 1, :, cut[t]] = (r * inverse[x, :, cut[t]]) * (1.0 / CHEB_CENTER)
            return carry

        lax.fori_loop(0, cells_x, first, 0, unroll=True)

    total_copy = pltpu.make_async_copy(total, total_hbm, sems.at[3])
    total_copy.start()

    y_wide = lax.broadcasted_iota(jnp.int32, (subs, width), 1) % side
    lower = lax.broadcasted_iota(jnp.int32, (rows, LANES), 1) < HALF
    sums = []
    for c in range(cases):
        sums_y = jnp.zeros((rows, 2 * LANES), F32)
        for piece in split_two(side_y[c]):
            sums_y = sums_y + jnp.dot(piece, fold_y_ref[...], preferred_element_type=F32)
        sums_x = []
        for e, x in enumerate((0, cells_x - 1)):
            at_ply = edge_x[e] * (side_x[c, e] - total[c, x])
            folded = jnp.zeros((rows, LANES), F32)
            for piece in split_two(at_ply):
                wide = piece.astype(F32)
                tall = jnp.concatenate(
                    [jnp.where(y_wide == q, wide, 0.0) for q in range(side)], axis=0
                ).astype(BF16)
                folded = folded + jnp.dot(tall, fold_ref[...], preferred_element_type=F32)
            sums_x.append(folded)
        sums.append(sums_x + [sums_y[:, :LANES], sums_y[:, LANES:]])
    for e in range(4):
        both = jnp.where(lower, sums[0][e], pltpu.roll(sums[1][e], HALF, 1))
        bound[e * rows : (e + 1) * rows, :] = jnp.concatenate(split_two(both), axis=1)
    copies[2].wait()
    posted = jnp.dot(turned_hit_ref[...], bound[...], preferred_element_type=F32)
    slots[...] = posted[:, :LANES] + posted[:, LANES:]
    pack_slots(slots, out_ref, peers, slot_depth)
    total_copy.wait()


def solve_block(packed, ready, peers, slot_depth, side):
    cases, cells_x, subs, width = ready[1].shape
    vm = pl.BlockSpec(memory_space=pltpu.VMEM)
    hbm = pl.BlockSpec(memory_space=pltpu.HBM)
    out_rows = peers * packed_rows(slot_depth)
    planes = (cells_x, subs, width)
    return pl.pallas_call(
        functools.partial(solve_kernel, peers=peers, slot_depth=slot_depth, side=side),
        out_shape=(
            jax.ShapeDtypeStruct((cases,) + planes, F32),
            jax.ShapeDtypeStruct((out_rows, LANES), F32),
        ),
        in_specs=[vm] + [hbm] * 3 + [vm] * 5,
        out_specs=(hbm, vm),
        scratch_shapes=[
            pltpu.VMEM(ready[0].shape, F32),
            pltpu.VMEM(ready[1].shape, F32),
            pltpu.VMEM(ready[2].shape, BF16),
            pltpu.VMEM((cases,) + planes, F32),
            pltpu.VMEM((peers * slot_depth, LANES), F32),
            pltpu.VMEM((4 * side * subs, 2 * LANES), BF16),
            pltpu.VMEM((2, cases, cells_x + 2, subs, width), F32),
            pltpu.VMEM((cases,) + planes, F32),
            pltpu.VMEM((cases, cells_x * subs, width), F32),
            pltpu.VMEM((cases, 2, subs, width), F32),
            pltpu.SemaphoreType.DMA((4,)),
        ],
        name="solve_block",
    )(packed, *ready)


def per_device(shell_state, source, knockdown, orient, active, point_owner, owner_nodes):
    cases, subs, side_x, width = source.shape
    plies = orient.shape[1]
    side = width // plies
    node_local = shell_state.shape[2]
    _, peers, slot_depth = owner_nodes.shape
    axes = ("grp", "sub")
    per_peer = packed_rows(slot_depth)

    nodes = owner_nodes.reshape(peers, slot_depth)
    picked = gather_shell(shell_state.reshape(cases * plies, node_local), nodes)
    arrived = lax.all_to_all(
        picked.reshape(peers, per_peer, LANES), axes, split_axis=0, concat_axis=0, tiled=True
    )

    owners = point_owner.reshape(-1)
    place = jnp.arange(owners.shape[0])
    earlier = (owners[:, None] == owners[None, :]) & (place[None, :] < place[:, None])
    slot_index = owners * slot_depth + jnp.sum(earlier.astype(jnp.int32), axis=1)
    ready = prepare(source, knockdown, orient, active, slot_index, peers * slot_depth)

    planes, outbound = solve_block(
        arrived.reshape(peers * per_peer, LANES), ready, peers, slot_depth, side
    )
    returned = lax.all_to_all(
        outbound.reshape(peers, per_peer, LANES), axes, split_axis=0, concat_axis=0, tiled=True
    )
    adjoint = jnp.transpose(planes, (0, 2, 1, 3))
    force = scatter_forces(
        returned.reshape(peers * per_peer, LANES), nodes, cases * plies, node_local
    )
    return adjoint, force.reshape(cases, plies, node_local)


def solution(mesh):
    in_specs = (
        P(None, None, ("grp", "sub")),
        P(None, ("grp", "sub"), None, None),
        P(("grp", "sub"), None, None),
        P(("grp", "sub"), None),
        P(("grp", "sub")),
        P(("grp", "sub"), None),
        P(("grp", "sub"), None, None),
    )
    out_specs = (P(None, ("grp", "sub"), None, None), P(None, None, ("grp", "sub")))
    return jax.shard_map(
        per_device, mesh=mesh, in_specs=in_specs, out_specs=out_specs, check_vma=False
    )
```

```python
import functools
import math

import jax
import jax.numpy as jnp
from jax import lax
from jax.experimental import pallas as pl
from jax.experimental.pallas import tpu as pltpu
from jax.sharding import PartitionSpec as P

SWEEPS = 3
STEPS = 2

FIBER_COND = 1.0
TRANSVERSE = 0.25
THROUGH = 0.15
MASS_SHARE = 0.05
CHEB_CENTER = 1.02
CHEB_HALF = 0.98

LANES = 128
HALF = 64
F32 = jnp.float32
BF16 = jnp.bfloat16


def packed_rows(slot_depth):
    return slot_depth * 3 // 4 if slot_depth % 32 == 0 else slot_depth


def pack_slots(rows_ref, out_ref, peers, slot_depth):
    used = lax.broadcasted_iota(jnp.int32, (8, LANES), 1) % HALF < 48
    if slot_depth % 32:
        for g in range(peers * slot_depth // 8):
            part = slice(g * 8, g * 8 + 8)
            out_ref[part, :] = jnp.where(used, rows_ref[part, :], 0.0)
        return
    for g in range(peers * slot_depth // 32):
        extra = rows_ref[g * 32 + 24 : g * 32 + 32, :]
        for k in range(3):
            moved = pltpu.roll(extra, 48 - 16 * k, 1)
            own = rows_ref[g * 32 + 8 * k : g * 32 + 8 * k + 8, :]
            out_ref[g * 24 + 8 * k : g * 24 + 8 * k + 8, :] = jnp.where(used, own, moved)


def unpack_slots(packed_ref, rows_ref, peers, slot_depth):
    if slot_depth % 32:
        rows_ref[...] = packed_ref[...]
        return
    third = lax.broadcasted_iota(jnp.int32, (8, LANES), 1) % HALF // 16
    for g in range(peers * slot_depth // 32):
        parts = []
        for k in range(3):
            own = packed_ref[g * 24 + 8 * k : g * 24 + 8 * k + 8, :]
            rows_ref[g * 32 + 8 * k : g * 32 + 8 * k + 8, :] = own
            parts.append(pltpu.roll(own, LANES - 48 + 16 * k, 1))
        extra = jnp.where(third == 0, parts[0], jnp.where(third == 1, parts[1], parts[2]))
        rows_ref[g * 32 + 24 : g * 32 + 32, :] = extra


def gather_kernel(node_ref, shell_hbm, out_ref, shell, turned, rows, sems, *, peers, slot_depth):
    width, node_local = shell.shape
    chunks = sems.shape[0]
    chunk = node_local // chunks
    copies = []
    for i in range(chunks):
        part = slice(i * chunk, (i + 1) * chunk)
        copies.append(pltpu.make_async_copy(shell_hbm.at[:, part], shell.at[:, part], sems.at[i]))
        copies[i].start()
    gap = jnp.zeros((HALF - width // 2, LANES), F32)
    for i in range(chunks):
        copies[i].wait()
        for t in range(i * chunk // LANES, (i + 1) * chunk // LANES):
            tile = shell[:, t * LANES : (t + 1) * LANES]
            parts = [tile[: width // 2], gap, tile[width // 2 :], gap]
            turned[8 + t * LANES : 8 + (t + 1) * LANES, :] = jnp.concatenate(parts, axis=0).T
    turned[0:8, :] = turned[8:16, :]

    def pick(peer, carry):
        for u in range(slot_depth):
            slot = peer * slot_depth + u
            rows[pl.ds(slot, 1), :] = turned[pl.ds(node_ref[peer, u] + 8, 1), :]
        return carry

    lax.fori_loop(0, peers, pick, 0)
    pack_slots(rows, out_ref, peers, slot_depth)


def gather_shell(shell_flat, nodes):
    width, node_local = shell_flat.shape
    peers, slot_depth = nodes.shape
    chunks = 8
    out_rows = peers * packed_rows(slot_depth)
    return pl.pallas_call(
        functools.partial(gather_kernel, peers=peers, slot_depth=slot_depth),
        out_shape=jax.ShapeDtypeStruct((out_rows, LANES), F32),
        in_specs=[
            pl.BlockSpec(memory_space=pltpu.SMEM),
            pl.BlockSpec(memory_space=pltpu.HBM),
        ],
        out_specs=pl.BlockSpec(memory_space=pltpu.VMEM),
        scratch_shapes=[
            pltpu.VMEM((width, node_local), F32),
            pltpu.VMEM((node_local + 8, LANES), F32),
            pltpu.VMEM((peers * slot_depth, LANES), F32),
            pltpu.SemaphoreType.DMA((chunks,)),
        ],
        name="gather_shell",
    )(nodes, shell_flat)


def pair_kernel(node_turned_ref, node_row_ref, node_ref, same_ref, node_out_ref):
    depth, peers = node_turned_ref.shape
    node_out_ref[...] = node_ref[...]
    for peer in range(peers):
        column = node_turned_ref[:, peer : peer + 1]
        same_ref[peer * depth : (peer + 1) * depth, :] = jnp.where(
            column == node_row_ref[...], 1.0, 0.0
        ).astype(BF16)


def pair_slots(nodes):
    peers, slot_depth = nodes.shape
    slots = peers * slot_depth
    vm = pl.BlockSpec(memory_space=pltpu.VMEM)
    return pl.pallas_call(
        pair_kernel,
        out_shape=[
            jax.ShapeDtypeStruct((slots, slots), BF16),
            jax.ShapeDtypeStruct(nodes.shape, jnp.int32),
        ],
        in_specs=[vm] * 3,
        out_specs=[vm] * 2,
        compiler_params=pltpu.CompilerParams(vmem_limit_bytes=16 << 20),
        cost_estimate=pl.CostEstimate(
            flops=4_000_000, bytes_accessed=4_000_000, transcendentals=0
        ),
        name="pair_slots",
    )(nodes.T, nodes.reshape(1, slots), nodes)


def scatter_kernel(
    node_ref, same_ref, packed_ref, out_hbm, total, rows, out, sems, *, peers, slot_depth
):
    width, node_local = out.shape
    unpack_slots(packed_ref, rows, peers, slot_depth)
    pieces = jnp.concatenate(split_two(rows[...]), axis=1)
    zero = jnp.zeros((LANES, LANES), F32)
    for t in range(node_local // LANES):
        total[8 + t * LANES : 8 + (t + 1) * LANES, :] = zero
    summed = jnp.dot(same_ref[...], pieces, preferred_element_type=F32)
    rows[...] = summed[:, :LANES] + summed[:, LANES:]

    def put(peer, carry):
        for u in range(slot_depth):
            slot = peer * slot_depth + u
            total[pl.ds(node_ref[peer, u] + 8, 1), :] = rows[pl.ds(slot, 1), :]
        return carry

    lax.fori_loop(0, peers, put, 0)

    chunks = sems.shape[0]
    chunk = node_local // chunks
    copies = []
    for i in range(chunks):
        for t in range(i * chunk // LANES, (i + 1) * chunk // LANES):
            tile = total[8 + t * LANES : 8 + (t + 1) * LANES, :].T
            out[: width // 2, t * LANES : (t + 1) * LANES] = tile[: width // 2]
            out[width // 2 :, t * LANES : (t + 1) * LANES] = tile[HALF : HALF + width // 2]
        part = slice(i * chunk, (i + 1) * chunk)
        copies.append(pltpu.make_async_copy(out.at[:, part], out_hbm.at[:, part], sems.at[i]))
        copies[i].start()
    for copy in copies:
        copy.wait()


def scatter_forces(packed, same, nodes, width, node_local):
    peers, slot_depth = nodes.shape
    chunks = 8
    vm = pl.BlockSpec(memory_space=pltpu.VMEM)
    return pl.pallas_call(
        functools.partial(scatter_kernel, peers=peers, slot_depth=slot_depth),
        out_shape=jax.ShapeDtypeStruct((width, node_local), F32),
        in_specs=[pl.BlockSpec(memory_space=pltpu.SMEM), vm, vm],
        out_specs=pl.BlockSpec(memory_space=pltpu.HBM),
        scratch_shapes=[
            pltpu.VMEM((node_local + 8, LANES), F32),
            pltpu.VMEM((peers * slot_depth, LANES), F32),
            pltpu.VMEM((width, node_local), F32),
            pltpu.SemaphoreType.DMA((chunks,)),
        ],
        compiler_params=pltpu.CompilerParams(vmem_limit_bytes=40 << 20),
        name="scatter_forces",
    )(nodes, same, packed)


def split_two(value):
    high = value.astype(BF16)
    return high, (value - high.astype(F32)).astype(BF16)


def from_lower_ply(values, low_ply, side):
    turned = [pltpu.roll(v, side, 1) for v in values]
    return [jnp.where(low_ply, turned[t - 1], turned[t]) for t in range(len(values))]


def from_upper_ply(values, high_ply, side):
    turned = [pltpu.roll(v, LANES - side, 1) for v in values]
    return [
        jnp.where(high_ply, turned[t + 1], turned[t]) for t in range(len(values) - 1)
    ] + [turned[-1]]


def ply_spread(tall, width, side):
    row = lax.broadcasted_iota(jnp.int32, (tall, width), 0)
    cell = lax.broadcasted_iota(jnp.int32, (tall, width), 1)
    return row, cell % side, row % HALF == cell // side


def indicator(condition):
    return jnp.where(condition, 1.0, 0.0).astype(BF16)


def prepare_kernel(
    active_ref, source_ref, knock_ref, cosine_ref, planes_hbm,
    planes, src, knock, ply_ref, sems, *, plies, side,
):
    cases, subs, cells_x, width = source_ref.shape
    tiles = width // LANES
    lane = lax.broadcasted_iota(jnp.int32, (subs, LANES), 1)
    y_place = lane % side
    first_y = y_place == 0
    last_y = y_place == side - 1
    low_ply = lane < side
    high_ply = lane >= LANES - side
    cut = [slice(t * LANES, (t + 1) * LANES) for t in range(tiles)]

    ply = lax.broadcasted_iota(jnp.int32, (subs, plies), 1)
    sub = lax.broadcasted_iota(jnp.int32, (subs, plies), 0)
    present = jnp.zeros((subs, plies), jnp.int32)
    for s in range(subs):
        present = jnp.where(sub == s, active_ref[s], present)
    mask = jnp.where(ply < present, 1.0, 0.0)
    upper = jnp.where((ply + 1 < present) & (ply + 1 < plies), 0.5, 0.0)
    cos_square = cosine_ref[...]
    terms = jnp.concatenate(
        [
            (FIBER_COND * cos_square + TRANSVERSE * (1.0 - cos_square)) * mask,
            (FIBER_COND * (1.0 - cos_square) + TRANSVERSE * cos_square) * mask,
            mask,
            upper,
        ],
        axis=0,
    )
    high, low = split_two(terms)
    only = indicator(ply_spread(plies, width, side)[2])
    spread_terms = jnp.dot(high, only, preferred_element_type=F32) + jnp.dot(
        low, only, preferred_element_type=F32
    )
    for k in range(4):
        ply_ref[k] = spread_terms[k * subs : (k + 1) * subs, :]

    for s in range(subs):
        for t in range(tiles):
            knock[t, s * cells_x : (s + 1) * cells_x, :] = knock_ref[s, :, cut[t]].astype(F32)
            for c in range(cases):
                at = (c * subs + s) * cells_x
                src[t, at : at + cells_x, :] = source_ref[c, s, :, cut[t]].astype(F32)

    def plane(ref, x, base=0):
        return [ref[t, pl.ds(base + x, subs, stride=cells_x), :] for t in range(tiles)]

    face_x, face_y, face_p, diag, inverse, along_y = (planes.at[k] for k in range(6))
    face_x[0] = jnp.zeros((subs, width), F32)
    face_x[cells_x] = jnp.zeros((subs, width), F32)

    def faces_x(x, carry):
        here = plane(knock, x)
        there = plane(knock, x + 1)
        for t in range(tiles):
            fiber = ply_ref[0, :, cut[t]]
            face_x[x + 1, :, cut[t]] = 0.5 * (here[t] * fiber + there[t] * fiber)
        return carry

    lax.fori_loop(0, cells_x - 1, faces_x, 0, unroll=5)

    def coefficients(x, carry):
        k = plane(knock, x)
        ax = [k[t] * ply_ref[0, :, cut[t]] for t in range(tiles)]
        ay = [k[t] * ply_ref[1, :, cut[t]] for t in range(tiles)]
        ac = [k[t] * (THROUGH * ply_ref[2, :, cut[t]]) for t in range(tiles)]
        up = from_upper_ply(ac, high_ply, side)
        fp = [ply_ref[3, :, cut[t]] * (ac[t] + up[t]) for t in range(tiles)]
        below = from_lower_ply(fp, low_ply, side)
        at_edge = jnp.where((x == 0) | (x == cells_x - 1), 1.0, 0.0)
        for t in range(tiles):
            fy = jnp.where(last_y, 0.0, 0.5 * (ay[t] + pltpu.roll(ay[t], LANES - 1, 1)))
            whole = (
                face_x[x, :, cut[t]]
                + face_x[x + 1, :, cut[t]]
                + pltpu.roll(fy, 1, 1)
                + fy
                + below[t]
                + fp[t]
                + at_edge * ax[t]
                + jnp.where(first_y | last_y, ay[t], 0.0)
                + MASS_SHARE * (ax[t] + ay[t] + ac[t])
                + (1.0 - ply_ref[2, :, cut[t]])
            )
            face_y[x, :, cut[t]] = fy
            face_p[x, :, cut[t]] = fp[t]
            diag[x, :, cut[t]] = whole
            inverse[x, :, cut[t]] = 1.0 / whole
            along_y[x, :, cut[t]] = ay[t]
            for c in range(cases):
                value = src[t, pl.ds(c * subs * cells_x + x, subs, stride=cells_x), :]
                planes[6 + c, x, :, cut[t]] = ply_ref[2, :, cut[t]] * value
        return carry

    for e, x in enumerate((0, cells_x - 1)):
        k = plane(knock, x)
        for t in range(tiles):
            planes[1 + e, cells_x, :, cut[t]] = k[t] * ply_ref[0, :, cut[t]]
    bands = sems.shape[0]
    band = cells_x // bands
    copies = []
    for i in range(bands):
        lax.fori_loop(i * band, (i + 1) * band, coefficients, 0, unroll=True)
        part = pl.ds(i * band, band + (1 if i == bands - 1 else 0))
        copies.append(
            pltpu.make_async_copy(planes.at[:, part], planes_hbm.at[:, part], sems.at[i])
        )
        copies[i].start()
    for copy in copies:
        copy.wait()


def prepare(source, knockdown, orient, active):
    cases, subs, cells_x, width = source.shape
    plies = orient.shape[1]
    side = width // plies
    cosine = jnp.cos(orient.astype(F32) * (math.pi / 6.0)) ** 2
    planes = (6 + cases, cells_x + 1, subs, width)
    vm = pl.BlockSpec(memory_space=pltpu.VMEM)
    return pl.pallas_call(
        functools.partial(prepare_kernel, plies=plies, side=side),
        out_shape=jax.ShapeDtypeStruct(planes, F32),
        in_specs=[pl.BlockSpec(memory_space=pltpu.SMEM)] + [vm] * 3,
        out_specs=pl.BlockSpec(memory_space=pltpu.HBM),
        scratch_shapes=[
            pltpu.VMEM(planes, F32),
            pltpu.VMEM((width // LANES, cases * subs * cells_x, LANES), F32),
            pltpu.VMEM((width // LANES, subs * cells_x, LANES), F32),
            pltpu.VMEM((4, subs, width), F32),
            pltpu.SemaphoreType.DMA((4,)),
        ],
        compiler_params=pltpu.CompilerParams(vmem_limit_bytes=58 << 20),
        cost_estimate=pl.CostEstimate(
            flops=40_000_000, bytes_accessed=12_000_000, transcendentals=0
        ),
        name="prepare",
    )(active, source, knockdown, cosine)


def solve_kernel(
    packed_ref, planes_hbm, slot_ref, slot_row_ref, total_hbm, out_ref,
    planes, total, slots, hit, bound, work, resid, side_y, side_x, tall, sems,
    *, peers, slot_depth, side,
):
    cases, cells_x, subs, width = total.shape
    parts = [slice(4, 6 + cases), slice(1, 3), slice(0, 1), slice(3, 4)]
    copies = [
        pltpu.make_async_copy(planes_hbm.at[part], planes.at[part], sems.at[k])
        for k, part in enumerate(parts)
    ]
    for copy in copies:
        copy.start()
    face_x, face_y, face_p, diag, inverse, along_y = (planes.at[k] for k in range(6))
    tiles = width // LANES
    lane = lax.broadcasted_iota(jnp.int32, (subs, LANES), 1)
    y_place = lane % side
    low_ply = lane < side
    high_ply = lane >= LANES - side
    cut = [slice(t * LANES, (t + 1) * LANES) for t in range(tiles)]

    zero = jnp.zeros((subs, width), F32)
    for k in range(2):
        for c in range(cases):
            work[k, c, 0] = zero
            work[k, c, cells_x + 1] = zero

    unpack_slots(packed_ref, slots, peers, slot_depth)
    pieces = jnp.concatenate(split_two(slots[...]), axis=1)
    slot_lane = lax.broadcasted_iota(jnp.int32, (subs, peers * slot_depth), 1)
    for pair in range(2 * side):
        both = [
            jnp.where(slot_lane == slot_ref[:, q : q + 1], 1.0, 0.0)
            for q in (2 * pair, 2 * pair + 1)
        ]
        hit[pair * 2 * subs : (pair + 1) * 2 * subs, :] = jnp.concatenate(both, axis=0).astype(BF16)
    found = jnp.dot(hit[...], pieces, preferred_element_type=F32)
    rows = side * subs
    lower = lax.broadcasted_iota(jnp.int32, (4 * rows, LANES), 1) < HALF
    high, low = found[:, :LANES], found[:, LANES:]
    bound[0] = jnp.where(lower, high, pltpu.roll(low, HALF, 1)).astype(BF16)
    bound[1] = jnp.where(lower, pltpu.roll(high, HALF, 1), low).astype(BF16)

    ends_x = jnp.concatenate([bound[c, : 2 * rows, :] for c in range(cases)], axis=0)
    ends_y = jnp.concatenate(
        [
            jnp.concatenate([bound[c, 2 * rows : 3 * rows, :], bound[c, 3 * rows :, :]], axis=1)
            for c in range(cases)
        ],
        axis=0,
    )
    spread_x = indicator(ply_spread(LANES, width, side)[2])
    row, y_cell, own = ply_spread(2 * LANES, width, side)
    spread_y = indicator(own & (y_cell == jnp.where(row < LANES, 0, side - 1)))
    spread = jnp.dot(ends_x, spread_x, preferred_element_type=F32)
    side_y[...] = jnp.dot(ends_y, spread_y, preferred_element_type=F32)
    for c in range(cases):
        for e in range(2):
            base = (2 * c + e) * rows
            for t in range(tiles):
                gathered = spread[base : base + subs, cut[t]]
                for q in range(1, side):
                    part = spread[base + q * subs : base + (q + 1) * subs, cut[t]]
                    gathered = jnp.where(y_place == q, part, gathered)
                side_x[c, e, :, cut[t]] = gathered
    copies[0].wait()
    copies[1].wait()

    def residual(x, carry):
        at_first = jnp.where(x == 0, 1.0, 0.0)
        at_final = jnp.where(x == cells_x - 1, 1.0, 0.0)
        row = pl.multiple_of(x * subs, subs)
        for c in range(cases):
            for t in range(tiles):
                value = (
                    planes[6 + c, x, :, cut[t]]
                    + along_y[x, :, cut[t]] * side_y[pl.ds(c * rows + row, subs), cut[t]]
                    + at_first * (planes[1, cells_x, :, cut[t]] * side_x[c, 0, :, cut[t]])
                    + at_final * (planes[2, cells_x, :, cut[t]] * side_x[c, 1, :, cut[t]])
                )
                resid[c, x, :, cut[t]] = value
                work[0, c, x + 1, :, cut[t]] = (value * inverse[x, :, cut[t]]) * (1.0 / CHEB_CENTER)
        return carry

    lax.fori_loop(0, cells_x, residual, 0, unroll=4)
    copies[2].wait()
    copies[3].wait()

    def operate(x, c, old):
        w = [work[old, c, x + 1, :, cut[t]] for t in range(tiles)]
        fp = [face_p[x, :, cut[t]] for t in range(tiles)]
        below = from_lower_ply([fp[t] * w[t] for t in range(tiles)], low_ply, side)
        above = from_upper_ply(w, high_ply, side)
        out = []
        for t in range(tiles):
            fy = face_y[x, :, cut[t]]
            beside = (
                face_x[x, :, cut[t]] * work[old, c, x, :, cut[t]]
                + face_x[x + 1, :, cut[t]] * work[old, c, x + 2, :, cut[t]]
                + pltpu.roll(fy * w[t], 1, 1)
                + fy * pltpu.roll(w[t], LANES - 1, 1)
                + (below[t] + fp[t] * above[t])
            )
            out.append(diag[x, :, cut[t]] * w[t] - beside)
        return w, out

    sigma = CHEB_CENTER / CHEB_HALF
    rho_first = 1.0 / sigma
    rho_next = 1.0 / (2.0 * sigma - rho_first)
    keep = rho_next * rho_first
    gain = 2.0 * rho_next / CHEB_HALF

    for sweep in range(SWEEPS):
        final = sweep == SWEEPS - 1

        def second(x, carry, sweep=sweep, final=final):
            for c in range(cases):
                w, moved = operate(x, c, 0)
                for t in range(tiles):
                    r = resid[c, x, :, cut[t]] - moved[t]
                    later = keep * w[t] + gain * (r * inverse[x, :, cut[t]])
                    sums = w[t] + later
                    if sweep:
                        sums = total[c, x, :, cut[t]] + sums
                    total[c, x, :, cut[t]] = sums
                    if not final:
                        resid[c, x, :, cut[t]] = r
                        work[1, c, x + 1, :, cut[t]] = later
                    else:
                        row = pl.multiple_of(x * subs, subs)
                        side_y[pl.ds(c * rows + row, subs), cut[t]] = along_y[x, :, cut[t]] * (
                            side_y[pl.ds(c * rows + row, subs), cut[t]] - sums
                        )
            return carry

        lax.fori_loop(0, cells_x, second, 0, unroll=True)
        if final:
            break

        def first(x, carry):
            for c in range(cases):
                _, moved = operate(x, c, 1)
                for t in range(tiles):
                    r = resid[c, x, :, cut[t]] - moved[t]
                    resid[c, x, :, cut[t]] = r
                    work[0, c, x + 1, :, cut[t]] = (r * inverse[x, :, cut[t]]) * (1.0 / CHEB_CENTER)
            return carry

        lax.fori_loop(0, cells_x, first, 0, unroll=True)

    total_copy = pltpu.make_async_copy(total, total_hbm, sems.at[4])
    total_copy.start()

    y_wide = lax.broadcasted_iota(jnp.int32, (subs, width), 1) % side
    for c in range(cases):
        for e, x in enumerate((0, cells_x - 1)):
            at_ply = planes[1 + e, cells_x] * (side_x[c, e] - total[c, x])
            for k, piece in enumerate(split_two(at_ply)):
                wide = piece.astype(F32)
                at = ((2 * c + e) * 2 + k) * rows
                tall[at : at + rows, :] = jnp.concatenate(
                    [jnp.where(y_wide == q, wide, 0.0) for q in range(side)], axis=0
                ).astype(BF16)
    across_lanes = (((1,), (1,)), ((), ()))
    folded_x = lax.dot_general(tall[...], spread_x, across_lanes, preferred_element_type=F32)
    folded_y = lax.dot_general(
        jnp.concatenate(split_two(side_y[...]), axis=0),
        spread_y,
        across_lanes,
        preferred_element_type=F32,
    )
    folded_y = folded_y[: cases * rows] + folded_y[cases * rows :]
    sums = []
    for c in range(cases):
        own = [
            folded_x[4 * c * rows + 2 * e * rows : 4 * c * rows + (2 * e + 1) * rows]
            + folded_x[4 * c * rows + (2 * e + 1) * rows : 4 * c * rows + (2 * e + 2) * rows]
            for e in range(2)
        ]
        part = folded_y[c * rows : (c + 1) * rows]
        sums.append(own + [part[:, :LANES], part[:, LANES:]])
    both = [jnp.where(lower[:rows], sums[0][e], sums[1][e]) for e in range(4)]
    forces = jnp.concatenate(
        [jnp.concatenate(split_two(part), axis=1) for part in both], axis=0
    )
    turned_hit = indicator(
        lax.broadcasted_iota(jnp.int32, (peers * slot_depth, 4 * rows), 0) == slot_row_ref[...]
    )
    posted = jnp.dot(turned_hit, forces, preferred_element_type=F32)
    slots[...] = posted[:, :LANES] + posted[:, LANES:]
    pack_slots(slots, out_ref, peers, slot_depth)
    total_copy.wait()


def solve_block(packed, ready, slot_index, source, peers, slot_depth, side):
    cases, subs, cells_x, width = source.shape
    points = slot_index.shape[1]
    vm = pl.BlockSpec(memory_space=pltpu.VMEM)
    hbm = pl.BlockSpec(memory_space=pltpu.HBM)
    out_rows = peers * packed_rows(slot_depth)
    planes = (cells_x, subs, width)
    return pl.pallas_call(
        functools.partial(solve_kernel, peers=peers, slot_depth=slot_depth, side=side),
        out_shape=(
            jax.ShapeDtypeStruct((cases,) + planes, F32),
            jax.ShapeDtypeStruct((out_rows, LANES), F32),
        ),
        in_specs=[vm, hbm, vm, vm],
        out_specs=(hbm, vm),
        scratch_shapes=[
            pltpu.VMEM(ready.shape, F32),
            pltpu.VMEM((cases,) + planes, F32),
            pltpu.VMEM((peers * slot_depth, LANES), F32),
            pltpu.VMEM((points * subs, peers * slot_depth), BF16),
            pltpu.VMEM((cases, 4 * side * subs, LANES), BF16),
            pltpu.VMEM((2, cases, cells_x + 2, subs, width), F32),
            pltpu.VMEM((cases,) + planes, F32),
            pltpu.VMEM((cases * side * subs, width), F32),
            pltpu.VMEM((cases, 2, subs, width), F32),
            pltpu.VMEM((4 * cases * side * subs, width), BF16),
            pltpu.SemaphoreType.DMA((5,)),
        ],
        compiler_params=pltpu.CompilerParams(vmem_limit_bytes=51 << 20),
        name="solve_block",
    )(packed, ready, slot_index, slot_index.T.reshape(1, points * subs))


def per_device(shell_state, source, knockdown, orient, active, point_owner, owner_nodes):
    cases, subs, side_x, width = source.shape
    plies = orient.shape[1]
    side = width // plies
    node_local = shell_state.shape[2]
    _, peers, slot_depth = owner_nodes.shape
    axes = ("grp", "sub")
    per_peer = packed_rows(slot_depth)

    nodes = owner_nodes.reshape(peers, slot_depth)
    picked = gather_shell(shell_state.reshape(cases * plies, node_local), nodes)
    arrived = lax.all_to_all(
        picked.reshape(peers, per_peer, LANES), axes, split_axis=0, concat_axis=0, tiled=True
    )

    owners = point_owner.reshape(-1)
    place = jnp.arange(owners.shape[0])
    earlier = (owners[:, None] == owners[None, :]) & (place[None, :] < place[:, None])
    rank = jnp.sum(earlier.astype(jnp.int32), axis=1).reshape(point_owner.shape)
    slot_index = point_owner * slot_depth + rank
    ready = prepare(source, knockdown, orient, active)
    planes, outbound = solve_block(
        arrived.reshape(peers * per_peer, LANES), ready, slot_index, source, peers, slot_depth, side
    )
    returned = lax.all_to_all(
        outbound.reshape(peers, per_peer, LANES), axes, split_axis=0, concat_axis=0, tiled=True
    )
    late_nodes, planes = lax.optimization_barrier((nodes, planes))
    adjoint = jnp.transpose(planes, (0, 2, 1, 3))
    same, late_nodes = pair_slots(late_nodes)
    force = scatter_forces(
        returned.reshape(peers * per_peer, LANES), same, late_nodes, cases * plies, node_local
    )
    return adjoint, force.reshape(cases, plies, node_local)


def solution(mesh):
    in_specs = (
        P(None, None, ("grp", "sub")),
        P(None, ("grp", "sub"), None, None),
        P(("grp", "sub"), None, None),
        P(("grp", "sub"), None),
        P(("grp", "sub")),
        P(("grp", "sub"), None),
        P(("grp", "sub"), None, None),
    )
    out_specs = (P(None, ("grp", "sub"), None, None), P(None, None, ("grp", "sub")))
    return jax.shard_map(
        per_device, mesh=mesh, in_specs=in_specs, out_specs=out_specs, check_vma=False
    )
```

```python
import functools
import math

import jax
import jax.numpy as jnp
from jax import lax
from jax.experimental import pallas as pl
from jax.experimental.pallas import tpu as pltpu
from jax.sharding import PartitionSpec as P

SWEEPS = 3
STEPS = 2

FIBER_COND = 1.0
TRANSVERSE = 0.25
THROUGH = 0.15
MASS_SHARE = 0.05
CHEB_CENTER = 1.02
CHEB_HALF = 0.98

LANES = 128
HALF = 64
F32 = jnp.float32
BF16 = jnp.bfloat16


def packed_rows(slot_depth):
    return slot_depth * 3 // 4 if slot_depth % 32 == 0 else slot_depth


def pack_slots(rows_ref, out_ref, peers, slot_depth):
    used = lax.broadcasted_iota(jnp.int32, (8, LANES), 1) % HALF < 48
    if slot_depth % 32:
        for g in range(peers * slot_depth // 8):
            part = slice(g * 8, g * 8 + 8)
            out_ref[part, :] = jnp.where(used, rows_ref[part, :], 0.0)
        return
    for g in range(peers * slot_depth // 32):
        extra = rows_ref[g * 32 + 24 : g * 32 + 32, :]
        for k in range(3):
            moved = pltpu.roll(extra, 48 - 16 * k, 1)
            own = rows_ref[g * 32 + 8 * k : g * 32 + 8 * k + 8, :]
            out_ref[g * 24 + 8 * k : g * 24 + 8 * k + 8, :] = jnp.where(used, own, moved)


def unpack_slots(packed_ref, rows_ref, peers, slot_depth):
    if slot_depth % 32:
        rows_ref[...] = packed_ref[...]
        return
    third = lax.broadcasted_iota(jnp.int32, (8, LANES), 1) % HALF // 16
    for g in range(peers * slot_depth // 32):
        parts = []
        for k in range(3):
            own = packed_ref[g * 24 + 8 * k : g * 24 + 8 * k + 8, :]
            rows_ref[g * 32 + 8 * k : g * 32 + 8 * k + 8, :] = own
            parts.append(pltpu.roll(own, LANES - 48 + 16 * k, 1))
        extra = jnp.where(third == 0, parts[0], jnp.where(third == 1, parts[1], parts[2]))
        rows_ref[g * 32 + 24 : g * 32 + 32, :] = extra


def gather_kernel(node_ref, shell_hbm, out_ref, shell, turned, rows, sems, *, peers, slot_depth):
    width, node_local = shell.shape
    chunks = sems.shape[0]
    chunk = node_local // chunks
    copies = []
    for i in range(chunks):
        part = slice(i * chunk, (i + 1) * chunk)
        copies.append(pltpu.make_async_copy(shell_hbm.at[:, part], shell.at[:, part], sems.at[i]))
        copies[i].start()
    gap = jnp.zeros((HALF - width // 2, LANES), F32)
    for i in range(chunks):
        copies[i].wait()
        for t in range(i * chunk // LANES, (i + 1) * chunk // LANES):
            tile = shell[:, t * LANES : (t + 1) * LANES]
            parts = [tile[: width // 2], gap, tile[width // 2 :], gap]
            turned[8 + t * LANES : 8 + (t + 1) * LANES, :] = jnp.concatenate(parts, axis=0).T
    turned[0:8, :] = turned[8:16, :]

    def pick(peer, carry):
        for u in range(slot_depth):
            slot = peer * slot_depth + u
            rows[pl.ds(slot, 1), :] = turned[pl.ds(node_ref[peer, u] + 8, 1), :]
        return carry

    lax.fori_loop(0, peers, pick, 0, unroll=4)
    pack_slots(rows, out_ref, peers, slot_depth)


def gather_shell(shell_flat, nodes):
    width, node_local = shell_flat.shape
    peers, slot_depth = nodes.shape
    chunks = 8
    out_rows = peers * packed_rows(slot_depth)
    return pl.pallas_call(
        functools.partial(gather_kernel, peers=peers, slot_depth=slot_depth),
        out_shape=jax.ShapeDtypeStruct((out_rows, LANES), F32),
        in_specs=[
            pl.BlockSpec(memory_space=pltpu.SMEM),
            pl.BlockSpec(memory_space=pltpu.HBM),
        ],
        out_specs=pl.BlockSpec(memory_space=pltpu.VMEM),
        scratch_shapes=[
            pltpu.VMEM((width, node_local), F32),
            pltpu.VMEM((node_local + 8, LANES), F32),
            pltpu.VMEM((peers * slot_depth, LANES), F32),
            pltpu.SemaphoreType.DMA((chunks,)),
        ],
        name="gather_shell",
    )(nodes, shell_flat)


def pair_kernel(node_turned_ref, node_row_ref, node_ref, same_ref, node_out_ref):
    depth, peers = node_turned_ref.shape
    node_out_ref[...] = node_ref[...]
    for peer in range(peers):
        column = node_turned_ref[:, peer : peer + 1]
        same_ref[peer * depth : (peer + 1) * depth, :] = jnp.where(
            column == node_row_ref[...], 1.0, 0.0
        ).astype(BF16)


def pair_slots(nodes):
    peers, slot_depth = nodes.shape
    slots = peers * slot_depth
    vm = pl.BlockSpec(memory_space=pltpu.VMEM)
    return pl.pallas_call(
        pair_kernel,
        out_shape=[
            jax.ShapeDtypeStruct((slots, slots), BF16),
            jax.ShapeDtypeStruct(nodes.shape, jnp.int32),
        ],
        in_specs=[vm] * 3,
        out_specs=[vm] * 2,
        compiler_params=pltpu.CompilerParams(vmem_limit_bytes=16 << 20),
        cost_estimate=pl.CostEstimate(
            flops=4_000_000, bytes_accessed=4_000_000, transcendentals=0
        ),
        name="pair_slots",
    )(nodes.T, nodes.reshape(1, slots), nodes)


def scatter_kernel(
    node_ref, same_ref, packed_ref, out_hbm, total, rows, out, sems, *, peers, slot_depth
):
    width, node_local = out.shape
    unpack_slots(packed_ref, rows, peers, slot_depth)
    pieces = jnp.concatenate(split_two(rows[...]), axis=1)
    zero = jnp.zeros((LANES, LANES), F32)
    for t in range(node_local // LANES):
        total[8 + t * LANES : 8 + (t + 1) * LANES, :] = zero
    summed = jnp.dot(same_ref[...], pieces, preferred_element_type=F32)
    rows[...] = summed[:, :LANES] + summed[:, LANES:]

    def put(peer, carry):
        for u in range(slot_depth):
            slot = peer * slot_depth + u
            total[pl.ds(node_ref[peer, u] + 8, 1), :] = rows[pl.ds(slot, 1), :]
        return carry

    lax.fori_loop(0, peers, put, 0, unroll=4)

    chunks = sems.shape[0]
    chunk = node_local // chunks
    copies = []
    for i in range(chunks):
        for t in range(i * chunk // LANES, (i + 1) * chunk // LANES):
            tile = total[8 + t * LANES : 8 + (t + 1) * LANES, :].T
            out[: width // 2, t * LANES : (t + 1) * LANES] = tile[: width // 2]
            out[width // 2 :, t * LANES : (t + 1) * LANES] = tile[HALF : HALF + width // 2]
        part = slice(i * chunk, (i + 1) * chunk)
        copies.append(pltpu.make_async_copy(out.at[:, part], out_hbm.at[:, part], sems.at[i]))
        copies[i].start()
    for copy in copies:
        copy.wait()


def scatter_forces(packed, same, nodes, width, node_local):
    peers, slot_depth = nodes.shape
    chunks = 8
    vm = pl.BlockSpec(memory_space=pltpu.VMEM)
    return pl.pallas_call(
        functools.partial(scatter_kernel, peers=peers, slot_depth=slot_depth),
        out_shape=jax.ShapeDtypeStruct((width, node_local), F32),
        in_specs=[pl.BlockSpec(memory_space=pltpu.SMEM), vm, vm],
        out_specs=pl.BlockSpec(memory_space=pltpu.HBM),
        scratch_shapes=[
            pltpu.VMEM((node_local + 8, LANES), F32),
            pltpu.VMEM((peers * slot_depth, LANES), F32),
            pltpu.VMEM((width, node_local), F32),
            pltpu.SemaphoreType.DMA((chunks,)),
        ],
        compiler_params=pltpu.CompilerParams(vmem_limit_bytes=40 << 20),
        name="scatter_forces",
    )(nodes, same, packed)


def split_two(value):
    high = value.astype(BF16)
    return high, (value - high.astype(F32)).astype(BF16)


def ply_of(cell, width, side):
    return cell % LANES // side * (width // LANES) + cell // LANES


def from_lower_ply(values, side):
    return [pltpu.roll(values[-1], side, 1)] + values[:-1]


def from_upper_ply(values, side):
    return values[1:] + [pltpu.roll(values[0], LANES - side, 1)]


def ply_spread(tall, width, side):
    row = lax.broadcasted_iota(jnp.int32, (tall, width), 0)
    cell = lax.broadcasted_iota(jnp.int32, (tall, width), 1)
    return row, cell % side, row % HALF == ply_of(cell, width, side)


def indicator(condition):
    return jnp.where(condition, 1.0, 0.0).astype(BF16)


def prepare_kernel(
    active_ref, source_ref, knock_ref, cosine_ref, planes_hbm,
    planes, src, knock, ply_ref, sems, *, plies, side,
):
    cases, subs, cells_x, width = source_ref.shape
    tiles = width // LANES
    lane = lax.broadcasted_iota(jnp.int32, (subs, LANES), 1)
    y_place = lane % side
    first_y = y_place == 0
    last_y = y_place == side - 1
    cut = [slice(t * LANES, (t + 1) * LANES) for t in range(tiles)]

    ply = lax.broadcasted_iota(jnp.int32, (subs, plies), 1)
    sub = lax.broadcasted_iota(jnp.int32, (subs, plies), 0)
    present = jnp.zeros((subs, plies), jnp.int32)
    for s in range(subs):
        present = jnp.where(sub == s, active_ref[s], present)
    mask = jnp.where(ply < present, 1.0, 0.0)
    upper = jnp.where((ply + 1 < present) & (ply + 1 < plies), 0.5, 0.0)
    cos_square = cosine_ref[...]
    terms = jnp.concatenate(
        [
            (FIBER_COND * cos_square + TRANSVERSE * (1.0 - cos_square)) * mask,
            (FIBER_COND * (1.0 - cos_square) + TRANSVERSE * cos_square) * mask,
            mask,
            upper,
        ],
        axis=0,
    )
    high, low = split_two(terms)
    only = indicator(ply_spread(plies, width, side)[2])
    spread_terms = jnp.dot(high, only, preferred_element_type=F32) + jnp.dot(
        low, only, preferred_element_type=F32
    )
    for k in range(4):
        ply_ref[k] = spread_terms[k * subs : (k + 1) * subs, :]

    natural = lax.broadcasted_iota(jnp.int32, (width, width), 0)
    cell = lax.broadcasted_iota(jnp.int32, (width, width), 1)
    order = indicator(natural == ply_of(cell, width, side) * side + cell % side)
    for ref, into in ((source_ref, src), (knock_ref, knock)):
        ordered = jnp.dot(ref[...].reshape(-1, width), order, preferred_element_type=F32)
        for t in range(tiles):
            into[t] = ordered[:, cut[t]]

    def plane(ref, x, base=0):
        return [ref[t, pl.ds(base + x, subs, stride=cells_x), :] for t in range(tiles)]

    face_x, face_y, face_p, diag, inverse, along_y = (planes.at[k] for k in range(6))
    face_x[0] = jnp.zeros((subs, width), F32)
    face_x[cells_x] = jnp.zeros((subs, width), F32)

    def faces_x(x, carry):
        here = plane(knock, x)
        there = plane(knock, x + 1)
        for t in range(tiles):
            fiber = ply_ref[0, :, cut[t]]
            face_x[x + 1, :, cut[t]] = 0.5 * (here[t] * fiber + there[t] * fiber)
        return carry

    lax.fori_loop(0, cells_x - 1, faces_x, 0, unroll=5)

    def coefficients(x, carry):
        k = plane(knock, x)
        ax = [k[t] * ply_ref[0, :, cut[t]] for t in range(tiles)]
        ay = [k[t] * ply_ref[1, :, cut[t]] for t in range(tiles)]
        ac = [k[t] * (THROUGH * ply_ref[2, :, cut[t]]) for t in range(tiles)]
        up = from_upper_ply(ac, side)
        fp = [ply_ref[3, :, cut[t]] * (ac[t] + up[t]) for t in range(tiles)]
        below = from_lower_ply(fp, side)
        at_edge = jnp.where((x == 0) | (x == cells_x - 1), 1.0, 0.0)
        for t in range(tiles):
            fy = jnp.where(last_y, 0.0, 0.5 * (ay[t] + pltpu.roll(ay[t], LANES - 1, 1)))
            whole = (
                face_x[x, :, cut[t]]
                + face_x[x + 1, :, cut[t]]
                + pltpu.roll(fy, 1, 1)
                + fy
                + below[t]
                + fp[t]
                + at_edge * ax[t]
                + jnp.where(first_y | last_y, ay[t], 0.0)
                + MASS_SHARE * (ax[t] + ay[t] + ac[t])
                + (1.0 - ply_ref[2, :, cut[t]])
            )
            face_y[x, :, cut[t]] = fy
            face_p[x, :, cut[t]] = fp[t]
            diag[x, :, cut[t]] = whole
            inverse[x, :, cut[t]] = 1.0 / whole
            along_y[x, :, cut[t]] = ay[t]
            for c in range(cases):
                value = src[t, pl.ds(c * subs * cells_x + x, subs, stride=cells_x), :]
                planes[6 + c, x, :, cut[t]] = ply_ref[2, :, cut[t]] * value
        return carry

    for e, x in enumerate((0, cells_x - 1)):
        k = plane(knock, x)
        for t in range(tiles):
            planes[1 + e, cells_x, :, cut[t]] = k[t] * ply_ref[0, :, cut[t]]
    bands = sems.shape[0]
    band = cells_x // bands
    copies = []
    for i in range(bands):
        lax.fori_loop(i * band, (i + 1) * band, coefficients, 0, unroll=True)
        part = pl.ds(i * band, band + (1 if i == bands - 1 else 0))
        copies.append(
            pltpu.make_async_copy(planes.at[:, part], planes_hbm.at[:, part], sems.at[i])
        )
        copies[i].start()
    for copy in copies:
        copy.wait()


def prepare(source, knockdown, orient, active):
    cases, subs, cells_x, width = source.shape
    plies = orient.shape[1]
    side = width // plies
    cosine = jnp.cos(orient.astype(F32) * (math.pi / 6.0)) ** 2
    planes = (6 + cases, cells_x + 1, subs, width)
    vm = pl.BlockSpec(memory_space=pltpu.VMEM)
    return pl.pallas_call(
        functools.partial(prepare_kernel, plies=plies, side=side),
        out_shape=jax.ShapeDtypeStruct(planes, F32),
        in_specs=[pl.BlockSpec(memory_space=pltpu.SMEM)] + [vm] * 3,
        out_specs=pl.BlockSpec(memory_space=pltpu.HBM),
        scratch_shapes=[
            pltpu.VMEM(planes, F32),
            pltpu.VMEM((width // LANES, cases * subs * cells_x, LANES), F32),
            pltpu.VMEM((width // LANES, subs * cells_x, LANES), F32),
            pltpu.VMEM((4, subs, width), F32),
            pltpu.SemaphoreType.DMA((4,)),
        ],
        compiler_params=pltpu.CompilerParams(vmem_limit_bytes=58 << 20),
        cost_estimate=pl.CostEstimate(
            flops=40_000_000, bytes_accessed=12_000_000, transcendentals=0
        ),
        name="prepare",
    )(active, source, knockdown, cosine)


def solve_kernel(
    packed_ref, planes_hbm, slot_ref, slot_row_ref, total, out_ref,
    planes, slots, hit, bound, work, resid, side_y, side_x, tall, sems,
    *, peers, slot_depth, side,
):
    cases, cells_x, subs, width = total.shape
    parts = [slice(4, 6 + cases), slice(1, 3), slice(0, 1), slice(3, 4)]
    copies = [
        pltpu.make_async_copy(planes_hbm.at[part], planes.at[part], sems.at[k])
        for k, part in enumerate(parts)
    ]
    for copy in copies:
        copy.start()
    face_x, face_y, face_p, diag, inverse, along_y = (planes.at[k] for k in range(6))
    tiles = width // LANES
    lane = lax.broadcasted_iota(jnp.int32, (subs, LANES), 1)
    y_place = lane % side
    cut = [slice(t * LANES, (t + 1) * LANES) for t in range(tiles)]

    zero = jnp.zeros((subs, width), F32)
    for k in range(2):
        for c in range(cases):
            work[k, c, 0] = zero
            work[k, c, cells_x + 1] = zero

    unpack_slots(packed_ref, slots, peers, slot_depth)
    pieces = jnp.concatenate(split_two(slots[...]), axis=1)
    slot_lane = lax.broadcasted_iota(jnp.int32, (subs, peers * slot_depth), 1)
    for pair in range(2 * side):
        both = [
            jnp.where(slot_lane == slot_ref[:, q : q + 1], 1.0, 0.0)
            for q in (2 * pair, 2 * pair + 1)
        ]
        hit[pair * 2 * subs : (pair + 1) * 2 * subs, :] = jnp.concatenate(both, axis=0).astype(BF16)
    found = jnp.dot(hit[...], pieces, preferred_element_type=F32)
    rows = side * subs
    lower = lax.broadcasted_iota(jnp.int32, (4 * rows, LANES), 1) < HALF
    high, low = found[:, :LANES], found[:, LANES:]
    bound[0] = jnp.where(lower, high, pltpu.roll(low, HALF, 1)).astype(BF16)
    bound[1] = jnp.where(lower, pltpu.roll(high, HALF, 1), low).astype(BF16)

    ends_x = jnp.concatenate([bound[c, : 2 * rows, :] for c in range(cases)], axis=0)
    ends_y = jnp.concatenate(
        [
            jnp.concatenate([bound[c, 2 * rows : 3 * rows, :], bound[c, 3 * rows :, :]], axis=1)
            for c in range(cases)
        ],
        axis=0,
    )
    spread_x = indicator(ply_spread(LANES, width, side)[2])
    row, y_cell, own = ply_spread(2 * LANES, width, side)
    spread_y = indicator(own & (y_cell == jnp.where(row < LANES, 0, side - 1)))
    spread = jnp.dot(ends_x, spread_x, preferred_element_type=F32)
    side_y[...] = jnp.dot(ends_y, spread_y, preferred_element_type=F32)
    for c in range(cases):
        for e in range(2):
            base = (2 * c + e) * rows
            for t in range(tiles):
                gathered = spread[base : base + subs, cut[t]]
                for q in range(1, side):
                    part = spread[base + q * subs : base + (q + 1) * subs, cut[t]]
                    gathered = jnp.where(y_place == q, part, gathered)
                side_x[c, e, :, cut[t]] = gathered
    copies[0].wait()
    copies[1].wait()

    def residual(x, carry):
        at_first = jnp.where(x == 0, 1.0, 0.0)
        at_final = jnp.where(x == cells_x - 1, 1.0, 0.0)
        row = pl.multiple_of(x * subs, subs)
        for c in range(cases):
            for t in range(tiles):
                value = (
                    planes[6 + c, x, :, cut[t]]
                    + along_y[x, :, cut[t]] * side_y[pl.ds(c * rows + row, subs), cut[t]]
                    + at_first * (planes[1, cells_x, :, cut[t]] * side_x[c, 0, :, cut[t]])
                    + at_final * (planes[2, cells_x, :, cut[t]] * side_x[c, 1, :, cut[t]])
                )
                resid[c, x, :, cut[t]] = value
                work[0, c, x + 1, :, cut[t]] = (value * inverse[x, :, cut[t]]) * (1.0 / CHEB_CENTER)
        return carry

    lax.fori_loop(0, cells_x, residual, 0, unroll=4)
    copies[2].wait()
    copies[3].wait()

    def operate(x, c, old):
        w = [work[old, c, x + 1, :, cut[t]] for t in range(tiles)]
        fp = [face_p[x, :, cut[t]] for t in range(tiles)]
        below = from_lower_ply([fp[t] * w[t] for t in range(tiles)], side)
        above = from_upper_ply(w, side)
        out = []
        for t in range(tiles):
            fy = face_y[x, :, cut[t]]
            beside = (
                face_x[x, :, cut[t]] * work[old, c, x, :, cut[t]]
                + face_x[x + 1, :, cut[t]] * work[old, c, x + 2, :, cut[t]]
                + pltpu.roll(fy * w[t], 1, 1)
                + fy * pltpu.roll(w[t], LANES - 1, 1)
                + (below[t] + fp[t] * above[t])
            )
            out.append(diag[x, :, cut[t]] * w[t] - beside)
        return w, out

    sigma = CHEB_CENTER / CHEB_HALF
    rho_first = 1.0 / sigma
    rho_next = 1.0 / (2.0 * sigma - rho_first)
    keep = rho_next * rho_first
    gain = 2.0 * rho_next / CHEB_HALF

    for sweep in range(SWEEPS):
        final = sweep == SWEEPS - 1

        def second(x, carry, sweep=sweep, final=final):
            for c in range(cases):
                w, moved = operate(x, c, 0)
                for t in range(tiles):
                    r = resid[c, x, :, cut[t]] - moved[t]
                    later = keep * w[t] + gain * (r * inverse[x, :, cut[t]])
                    sums = w[t] + later
                    if sweep:
                        sums = total[c, x, :, cut[t]] + sums
                    total[c, x, :, cut[t]] = sums
                    if not final:
                        resid[c, x, :, cut[t]] = r
                        work[1, c, x + 1, :, cut[t]] = later
                    else:
                        row = pl.multiple_of(x * subs, subs)
                        side_y[pl.ds(c * rows + row, subs), cut[t]] = along_y[x, :, cut[t]] * (
                            side_y[pl.ds(c * rows + row, subs), cut[t]] - sums
                        )
            return carry

        lax.fori_loop(0, cells_x, second, 0, unroll=True)
        if final:
            break

        def first(x, carry):
            for c in range(cases):
                _, moved = operate(x, c, 1)
                for t in range(tiles):
                    r = resid[c, x, :, cut[t]] - moved[t]
                    resid[c, x, :, cut[t]] = r
                    work[0, c, x + 1, :, cut[t]] = (r * inverse[x, :, cut[t]]) * (1.0 / CHEB_CENTER)
            return carry

        lax.fori_loop(0, cells_x, first, 0, unroll=True)

    y_wide = lax.broadcasted_iota(jnp.int32, (subs, width), 1) % side
    for c in range(cases):
        for e, x in enumerate((0, cells_x - 1)):
            at_ply = planes[1 + e, cells_x] * (side_x[c, e] - total[c, x])
            for k, piece in enumerate(split_two(at_ply)):
                wide = piece.astype(F32)
                at = ((2 * c + e) * 2 + k) * rows
                tall[at : at + rows, :] = jnp.concatenate(
                    [jnp.where(y_wide == q, wide, 0.0) for q in range(side)], axis=0
                ).astype(BF16)
    across_lanes = (((1,), (1,)), ((), ()))
    folded_x = lax.dot_general(tall[...], spread_x, across_lanes, preferred_element_type=F32)
    folded_y = lax.dot_general(
        jnp.concatenate(split_two(side_y[...]), axis=0),
        spread_y,
        across_lanes,
        preferred_element_type=F32,
    )
    folded_y = folded_y[: cases * rows] + folded_y[cases * rows :]
    sums = []
    for c in range(cases):
        own = [
            folded_x[4 * c * rows + 2 * e * rows : 4 * c * rows + (2 * e + 1) * rows]
            + folded_x[4 * c * rows + (2 * e + 1) * rows : 4 * c * rows + (2 * e + 2) * rows]
            for e in range(2)
        ]
        part = folded_y[c * rows : (c + 1) * rows]
        sums.append(own + [part[:, :LANES], part[:, LANES:]])
    both = [jnp.where(lower[:rows], sums[0][e], sums[1][e]) for e in range(4)]
    forces = jnp.concatenate(
        [jnp.concatenate(split_two(part), axis=1) for part in both], axis=0
    )
    turned_hit = indicator(
        lax.broadcasted_iota(jnp.int32, (peers * slot_depth, 4 * rows), 0) == slot_row_ref[...]
    )
    posted = jnp.dot(turned_hit, forces, preferred_element_type=F32)
    slots[...] = posted[:, :LANES] + posted[:, LANES:]
    pack_slots(slots, out_ref, peers, slot_depth)


def solve_block(packed, ready, slot_index, source, peers, slot_depth, side):
    cases, subs, cells_x, width = source.shape
    points = slot_index.shape[1]
    vm = pl.BlockSpec(memory_space=pltpu.VMEM)
    hbm = pl.BlockSpec(memory_space=pltpu.HBM)
    out_rows = peers * packed_rows(slot_depth)
    planes = (cells_x, subs, width)
    return pl.pallas_call(
        functools.partial(solve_kernel, peers=peers, slot_depth=slot_depth, side=side),
        out_shape=(
            jax.ShapeDtypeStruct((cases,) + planes, F32),
            jax.ShapeDtypeStruct((out_rows, LANES), F32),
        ),
        in_specs=[vm, hbm, vm, vm],
        out_specs=(vm, vm),
        scratch_shapes=[
            pltpu.VMEM(ready.shape, F32),
            pltpu.VMEM((peers * slot_depth, LANES), F32),
            pltpu.VMEM((points * subs, peers * slot_depth), BF16),
            pltpu.VMEM((cases, 4 * side * subs, LANES), BF16),
            pltpu.VMEM((2, cases, cells_x + 2, subs, width), F32),
            pltpu.VMEM((cases,) + planes, F32),
            pltpu.VMEM((cases * side * subs, width), F32),
            pltpu.VMEM((cases, 2, subs, width), F32),
            pltpu.VMEM((4 * cases * side * subs, width), BF16),
            pltpu.SemaphoreType.DMA((4,)),
        ],
        compiler_params=pltpu.CompilerParams(vmem_limit_bytes=51 << 20),
        name="solve_block",
    )(packed, ready, slot_index, slot_index.T.reshape(1, points * subs))


def finish_kernel(total_ref, adjoint_ref, turned, *, side):
    cases, cells_x, subs, width = total_ref.shape
    rows = cases * cells_x * subs
    value = total_ref[...].reshape(rows, width)
    high = value.astype(BF16)
    rest = value - high.astype(F32)
    middle, low = split_two(rest)
    cell = lax.broadcasted_iota(jnp.int32, (width, width), 0)
    natural = lax.broadcasted_iota(jnp.int32, (width, width), 1)
    order = indicator(natural == ply_of(cell, width, side) * side + cell % side)
    found = jnp.dot(
        jnp.concatenate([high, middle, low], axis=0), order, preferred_element_type=F32
    )
    found = (found[:rows] + found[rows : 2 * rows]) + found[2 * rows :]
    for t in range(width // LANES):
        cut = slice(t * LANES, (t + 1) * LANES)
        for c in range(cases):
            for x in range(cells_x):
                at = (c * cells_x + x) * subs
                turned[t, pl.ds(c * subs * cells_x + x, subs, stride=cells_x), :] = found[
                    at : at + subs, cut
                ]
        adjoint_ref[:, cut] = turned[t]


def finish(total, side):
    cases, cells_x, subs, width = total.shape
    rows = cases * cells_x * subs
    vm = pl.BlockSpec(memory_space=pltpu.VMEM)
    adjoint = pl.pallas_call(
        functools.partial(finish_kernel, side=side),
        out_shape=jax.ShapeDtypeStruct((rows, width), F32),
        in_specs=[vm],
        out_specs=vm,
        scratch_shapes=[pltpu.VMEM((width // LANES, rows, LANES), F32)],
        compiler_params=pltpu.CompilerParams(vmem_limit_bytes=24 << 20),
        cost_estimate=pl.CostEstimate(
            flops=10_000_000, bytes_accessed=8_000_000, transcendentals=0
        ),
        name="finish",
    )(total)
    return adjoint.reshape(cases, subs, cells_x, width)


def per_device(shell_state, source, knockdown, orient, active, point_owner, owner_nodes):
    cases, subs, side_x, width = source.shape
    plies = orient.shape[1]
    side = width // plies
    node_local = shell_state.shape[2]
    _, peers, slot_depth = owner_nodes.shape
    axes = ("grp", "sub")
    per_peer = packed_rows(slot_depth)

    nodes = owner_nodes.reshape(peers, slot_depth)
    picked = gather_shell(shell_state.reshape(cases * plies, node_local), nodes)
    arrived = lax.all_to_all(
        picked.reshape(peers, per_peer, LANES), axes, split_axis=0, concat_axis=0, tiled=True
    )

    owners = point_owner.reshape(-1)
    place = jnp.arange(owners.shape[0])
    earlier = (owners[:, None] == owners[None, :]) & (place[None, :] < place[:, None])
    rank = jnp.sum(earlier.astype(jnp.int32), axis=1).reshape(point_owner.shape)
    slot_index = point_owner * slot_depth + rank
    ready = prepare(source, knockdown, orient, active)
    planes, outbound = solve_block(
        arrived.reshape(peers * per_peer, LANES), ready, slot_index, source, peers, slot_depth, side
    )
    returned = lax.all_to_all(
        outbound.reshape(peers, per_peer, LANES), axes, split_axis=0, concat_axis=0, tiled=True
    )
    late_nodes, planes = lax.optimization_barrier((nodes, planes))
    adjoint = finish(planes, side)
    same, late_nodes = pair_slots(late_nodes)
    force = scatter_forces(
        returned.reshape(peers * per_peer, LANES), same, late_nodes, cases * plies, node_local
    )
    return adjoint, force.reshape(cases, plies, node_local)


def solution(mesh):
    in_specs = (
        P(None, None, ("grp", "sub")),
        P(None, ("grp", "sub"), None, None),
        P(("grp", "sub"), None, None),
        P(("grp", "sub"), None),
        P(("grp", "sub")),
        P(("grp", "sub"), None),
        P(("grp", "sub"), None, None),
    )
    out_specs = (P(None, ("grp", "sub"), None, None), P(None, None, ("grp", "sub")))
    return jax.shard_map(
        per_device, mesh=mesh, in_specs=in_specs, out_specs=out_specs, check_vma=False
    )
```

```python
import functools
import math

import jax
import jax.numpy as jnp
from jax import lax
from jax.experimental import pallas as pl
from jax.experimental.pallas import tpu as pltpu
from jax.sharding import PartitionSpec as P

SWEEPS = 3
STEPS = 2

FIBER_COND = 1.0
TRANSVERSE = 0.25
THROUGH = 0.15
MASS_SHARE = 0.05
CHEB_CENTER = 1.02
CHEB_HALF = 0.98

LANES = 128
HALF = 64
F32 = jnp.float32
BF16 = jnp.bfloat16


def packed_rows(slot_depth):
    return slot_depth * 3 // 4 if slot_depth % 32 == 0 else slot_depth


def pack_slots(rows_ref, out_ref, peers, slot_depth):
    used = lax.broadcasted_iota(jnp.int32, (8, LANES), 1) % HALF < 48
    if slot_depth % 32:
        for g in range(peers * slot_depth // 8):
            part = slice(g * 8, g * 8 + 8)
            out_ref[part, :] = jnp.where(used, rows_ref[part, :], 0.0)
        return
    for g in range(peers * slot_depth // 32):
        extra = rows_ref[g * 32 + 24 : g * 32 + 32, :]
        for k in range(3):
            moved = pltpu.roll(extra, 48 - 16 * k, 1)
            own = rows_ref[g * 32 + 8 * k : g * 32 + 8 * k + 8, :]
            out_ref[g * 24 + 8 * k : g * 24 + 8 * k + 8, :] = jnp.where(used, own, moved)


def unpack_slots(packed_ref, rows_ref, peers, slot_depth):
    if slot_depth % 32:
        rows_ref[...] = packed_ref[...]
        return
    third = lax.broadcasted_iota(jnp.int32, (8, LANES), 1) % HALF // 16
    for g in range(peers * slot_depth // 32):
        parts = []
        for k in range(3):
            own = packed_ref[g * 24 + 8 * k : g * 24 + 8 * k + 8, :]
            rows_ref[g * 32 + 8 * k : g * 32 + 8 * k + 8, :] = own
            parts.append(pltpu.roll(own, LANES - 48 + 16 * k, 1))
        extra = jnp.where(third == 0, parts[0], jnp.where(third == 1, parts[1], parts[2]))
        rows_ref[g * 32 + 24 : g * 32 + 32, :] = extra


def split_two(value):
    high = value.astype(BF16)
    return high, (value - high.astype(F32)).astype(BF16)


def indicator(condition):
    return jnp.where(condition, 1.0, 0.0).astype(BF16)


def gather_kernel(
    node_ref, shell_hbm, out_hbm, shell, turned, rows, packed, sems, out_sems, *, peers, slot_depth
):
    width, node_local = shell.shape
    chunks = sems.shape[0]
    chunk = node_local // chunks
    copies = []
    for i in range(chunks):
        part = slice(i * chunk, (i + 1) * chunk)
        copies.append(pltpu.make_async_copy(shell_hbm.at[:, part], shell.at[:, part], sems.at[i]))
        copies[i].start()
    gap = jnp.zeros((HALF - width // 2, LANES), F32)
    gap_two = jnp.zeros((HALF - width // 2, 2 * LANES), F32)
    unit_row = lax.broadcasted_iota(jnp.int32, (2 * LANES, 2 * LANES), 0)
    unit = indicator(unit_row == lax.broadcasted_iota(jnp.int32, (2 * LANES, 2 * LANES), 1))
    across_lanes = (((1,), (1,)), ((), ()))
    tiles = chunk // LANES
    in_matmul = tiles // 8 * 2
    for i in range(chunks):
        copies[i].wait()
        for t in range(i * tiles, i * tiles + in_matmul, 2):
            tile = shell[:, t * LANES : (t + 2) * LANES]
            both = jnp.concatenate(
                [tile[: width // 2], gap_two, tile[width // 2 :], gap_two], axis=0
            )
            pieces = jnp.concatenate(split_two(both), axis=0)
            out = lax.dot_general(unit, pieces, across_lanes, preferred_element_type=F32)
            turned[8 + t * LANES : 8 + (t + 2) * LANES, :] = out[:, :LANES] + out[:, LANES:]
        for t in range(i * tiles + in_matmul, (i + 1) * tiles):
            tile = shell[:, t * LANES : (t + 1) * LANES]
            parts = [tile[: width // 2], gap, tile[width // 2 :], gap]
            turned[8 + t * LANES : 8 + (t + 1) * LANES, :] = jnp.concatenate(parts, axis=0).T
    turned[0:8, :] = turned[8:16, :]

    def pick(peer, carry):
        for u in range(slot_depth):
            slot = peer * slot_depth + u
            rows[pl.ds(slot, 1), :] = turned[pl.ds(node_ref[peer, u] + 8, 1), :]
        return carry

    groups = out_sems.shape[0]
    share = peers // groups
    per_peer = packed_rows(slot_depth)
    sends = []
    for g in range(groups):
        lax.fori_loop(g * share, (g + 1) * share, pick, 0, unroll=4)
        own = slice(g * share * slot_depth, (g + 1) * share * slot_depth)
        part = slice(g * share * per_peer, (g + 1) * share * per_peer)
        pack_slots(rows.at[own], packed.at[part], share, slot_depth)
        sends.append(pltpu.make_async_copy(packed.at[part], out_hbm.at[part], out_sems.at[g]))
        sends[g].start()
    for send in sends:
        send.wait()


def gather_shell(shell_flat, nodes):
    width, node_local = shell_flat.shape
    peers, slot_depth = nodes.shape
    chunks, groups = 4, 8
    out_rows = peers * packed_rows(slot_depth)
    return pl.pallas_call(
        functools.partial(gather_kernel, peers=peers, slot_depth=slot_depth),
        out_shape=jax.ShapeDtypeStruct((out_rows, LANES), F32),
        in_specs=[
            pl.BlockSpec(memory_space=pltpu.SMEM),
            pl.BlockSpec(memory_space=pltpu.HBM),
        ],
        out_specs=pl.BlockSpec(memory_space=pltpu.HBM),
        scratch_shapes=[
            pltpu.VMEM((width, node_local), F32),
            pltpu.VMEM((node_local + 8, LANES), F32),
            pltpu.VMEM((peers * slot_depth, LANES), F32),
            pltpu.VMEM((out_rows, LANES), F32),
            pltpu.SemaphoreType.DMA((chunks,)),
            pltpu.SemaphoreType.DMA((groups,)),
        ],
        name="gather_shell",
    )(nodes, shell_flat)


def pair_kernel(node_turned_ref, node_row_ref, same_ref):
    depth, peers = node_turned_ref.shape
    for peer in range(peers):
        column = node_turned_ref[:, peer : peer + 1]
        same_ref[peer * depth : (peer + 1) * depth, :] = jnp.where(
            column == node_row_ref[...], 1.0, 0.0
        ).astype(BF16)


def pair_slots(nodes):
    peers, slot_depth = nodes.shape
    slots = peers * slot_depth
    vm = pl.BlockSpec(memory_space=pltpu.VMEM)
    return pl.pallas_call(
        pair_kernel,
        out_shape=jax.ShapeDtypeStruct((slots, slots), BF16),
        in_specs=[vm] * 2,
        out_specs=vm,
        compiler_params=pltpu.CompilerParams(vmem_limit_bytes=16 << 20),
        cost_estimate=pl.CostEstimate(
            flops=4_000_000, bytes_accessed=4_000_000, transcendentals=0
        ),
        name="pair_slots",
    )(nodes.T, nodes.reshape(1, slots))


def scatter_kernel(
    row_ref, same_ref, packed_ref, out_hbm, total, rows, out, sems, *, peers, slot_depth
):
    width, node_local = out.shape
    unpack_slots(packed_ref, rows, peers, slot_depth)
    pieces = jnp.concatenate(split_two(rows[...]), axis=1)
    zero = jnp.zeros((LANES, LANES), F32)
    for t in range(node_local // LANES):
        total[8 + t * LANES : 8 + (t + 1) * LANES, :] = zero
    summed = jnp.dot(same_ref[...], pieces, preferred_element_type=F32)
    rows[...] = summed[:, :LANES] + summed[:, LANES:]

    def put(group, carry):
        for u in range(LANES):
            slot = group * LANES + u
            total[pl.ds(row_ref[slot], 1), :] = rows[pl.ds(slot, 1), :]
        return carry

    lax.fori_loop(0, peers * slot_depth // LANES, put, 0)

    chunks = sems.shape[0]
    chunk = node_local // chunks
    copies = []
    for i in range(chunks):
        for t in range(i * chunk // LANES, (i + 1) * chunk // LANES):
            tile = total[8 + t * LANES : 8 + (t + 1) * LANES, :].T
            out[: width // 2, t * LANES : (t + 1) * LANES] = tile[: width // 2]
            out[width // 2 :, t * LANES : (t + 1) * LANES] = tile[HALF : HALF + width // 2]
        part = slice(i * chunk, (i + 1) * chunk)
        copies.append(pltpu.make_async_copy(out.at[:, part], out_hbm.at[:, part], sems.at[i]))
        copies[i].start()
    for copy in copies:
        copy.wait()


def scatter_forces(packed, same, node_rows, peers, slot_depth, width, node_local):
    chunks = 8
    vm = pl.BlockSpec(memory_space=pltpu.VMEM)
    return pl.pallas_call(
        functools.partial(scatter_kernel, peers=peers, slot_depth=slot_depth),
        out_shape=jax.ShapeDtypeStruct((width, node_local), F32),
        in_specs=[pl.BlockSpec(memory_space=pltpu.SMEM), vm, vm],
        out_specs=pl.BlockSpec(memory_space=pltpu.HBM),
        scratch_shapes=[
            pltpu.VMEM((node_local + 8, LANES), F32),
            pltpu.VMEM((peers * slot_depth, LANES), F32),
            pltpu.VMEM((width, node_local), F32),
            pltpu.SemaphoreType.DMA((chunks,)),
        ],
        compiler_params=pltpu.CompilerParams(vmem_limit_bytes=40 << 20),
        name="scatter_forces",
    )(node_rows, same, packed)


def ply_of(cell, width, side):
    return cell % LANES // side * (width // LANES) + cell // LANES


def from_lower_ply(values, side):
    return [pltpu.roll(values[-1], side, 1)] + values[:-1]


def from_upper_ply(values, side):
    return values[1:] + [pltpu.roll(values[0], LANES - side, 1)]


def ply_spread(tall, width, side):
    row = lax.broadcasted_iota(jnp.int32, (tall, width), 0)
    cell = lax.broadcasted_iota(jnp.int32, (tall, width), 1)
    return row, cell % side, row % HALF == ply_of(cell, width, side)


def prepare_kernel(
    active_ref, source_ref, knock_ref, cosine_ref, planes_hbm,
    planes, src, knock, ply_ref, sems, *, plies, side,
):
    cases, subs, cells_x, width = source_ref.shape
    tiles = width // LANES
    lane = lax.broadcasted_iota(jnp.int32, (subs, LANES), 1)
    y_place = lane % side
    first_y = y_place == 0
    last_y = y_place == side - 1
    cut = [slice(t * LANES, (t + 1) * LANES) for t in range(tiles)]

    ply = lax.broadcasted_iota(jnp.int32, (subs, plies), 1)
    sub = lax.broadcasted_iota(jnp.int32, (subs, plies), 0)
    present = jnp.zeros((subs, plies), jnp.int32)
    for s in range(subs):
        present = jnp.where(sub == s, active_ref[s], present)
    mask = jnp.where(ply < present, 1.0, 0.0)
    upper = jnp.where((ply + 1 < present) & (ply + 1 < plies), 0.5, 0.0)
    cos_square = cosine_ref[...]
    terms = jnp.concatenate(
        [
            (FIBER_COND * cos_square + TRANSVERSE * (1.0 - cos_square)) * mask,
            (FIBER_COND * (1.0 - cos_square) + TRANSVERSE * cos_square) * mask,
            mask,
            upper,
        ],
        axis=0,
    )
    high, low = split_two(terms)
    only = indicator(ply_spread(plies, width, side)[2])
    spread_terms = jnp.dot(high, only, preferred_element_type=F32) + jnp.dot(
        low, only, preferred_element_type=F32
    )
    for k in range(4):
        ply_ref[k] = spread_terms[k * subs : (k + 1) * subs, :]

    natural = lax.broadcasted_iota(jnp.int32, (width, width), 0)
    cell = lax.broadcasted_iota(jnp.int32, (width, width), 1)
    order = indicator(natural == ply_of(cell, width, side) * side + cell % side)
    for ref, into in ((source_ref, src), (knock_ref, knock)):
        ordered = jnp.dot(ref[...].reshape(-1, width), order, preferred_element_type=F32)
        for t in range(tiles):
            into[t] = ordered[:, cut[t]]

    def plane(ref, x, base=0):
        return [ref[t, pl.ds(base + x, subs, stride=cells_x), :] for t in range(tiles)]

    face_x, face_y, face_p, diag, inverse, along_y = (planes.at[k] for k in range(6))
    face_x[0] = jnp.zeros((subs, width), F32)
    face_x[cells_x] = jnp.zeros((subs, width), F32)

    def faces_x(x, carry):
        here = plane(knock, x)
        there = plane(knock, x + 1)
        for t in range(tiles):
            fiber = ply_ref[0, :, cut[t]]
            face_x[x + 1, :, cut[t]] = 0.5 * (here[t] * fiber + there[t] * fiber)
        return carry

    lax.fori_loop(0, cells_x - 1, faces_x, 0, unroll=5)

    def coefficients(x, carry):
        k = plane(knock, x)
        ax = [k[t] * ply_ref[0, :, cut[t]] for t in range(tiles)]
        ay = [k[t] * ply_ref[1, :, cut[t]] for t in range(tiles)]
        ac = [k[t] * (THROUGH * ply_ref[2, :, cut[t]]) for t in range(tiles)]
        up = from_upper_ply(ac, side)
        fp = [ply_ref[3, :, cut[t]] * (ac[t] + up[t]) for t in range(tiles)]
        below = from_lower_ply(fp, side)
        at_edge = jnp.where((x == 0) | (x == cells_x - 1), 1.0, 0.0)
        for t in range(tiles):
            fy = jnp.where(last_y, 0.0, 0.5 * (ay[t] + pltpu.roll(ay[t], LANES - 1, 1)))
            whole = (
                face_x[x, :, cut[t]]
                + face_x[x + 1, :, cut[t]]
                + pltpu.roll(fy, 1, 1)
                + fy
                + below[t]
                + fp[t]
                + at_edge * ax[t]
                + jnp.where(first_y | last_y, ay[t], 0.0)
                + MASS_SHARE * (ax[t] + ay[t] + ac[t])
                + (1.0 - ply_ref[2, :, cut[t]])
            )
            face_y[x, :, cut[t]] = fy
            face_p[x, :, cut[t]] = fp[t]
            diag[x, :, cut[t]] = whole
            inverse[x, :, cut[t]] = 1.0 / whole
            along_y[x, :, cut[t]] = ay[t]
            for c in range(cases):
                value = src[t, pl.ds(c * subs * cells_x + x, subs, stride=cells_x), :]
                planes[6 + c, x, :, cut[t]] = ply_ref[2, :, cut[t]] * value
        return carry

    for e, x in enumerate((0, cells_x - 1)):
        k = plane(knock, x)
        for t in range(tiles):
            planes[1 + e, cells_x, :, cut[t]] = k[t] * ply_ref[0, :, cut[t]]
    bands = sems.shape[0]
    band = cells_x // bands
    copies = []
    for i in range(bands):
        lax.fori_loop(i * band, (i + 1) * band, coefficients, 0, unroll=True)
        part = pl.ds(i * band, band + (1 if i == bands - 1 else 0))
        copies.append(
            pltpu.make_async_copy(planes.at[:, part], planes_hbm.at[:, part], sems.at[i])
        )
        copies[i].start()
    for copy in copies:
        copy.wait()


def prepare(source, knockdown, orient, active):
    cases, subs, cells_x, width = source.shape
    plies = orient.shape[1]
    side = width // plies
    cosine = jnp.cos(orient.astype(F32) * (math.pi / 6.0)) ** 2
    planes = (6 + cases, cells_x + 1, subs, width)
    vm = pl.BlockSpec(memory_space=pltpu.VMEM)
    return pl.pallas_call(
        functools.partial(prepare_kernel, plies=plies, side=side),
        out_shape=jax.ShapeDtypeStruct(planes, F32),
        in_specs=[pl.BlockSpec(memory_space=pltpu.SMEM)] + [vm] * 3,
        out_specs=pl.BlockSpec(memory_space=pltpu.HBM),
        scratch_shapes=[
            pltpu.VMEM(planes, F32),
            pltpu.VMEM((width // LANES, cases * subs * cells_x, LANES), F32),
            pltpu.VMEM((width // LANES, subs * cells_x, LANES), F32),
            pltpu.VMEM((4, subs, width), F32),
            pltpu.SemaphoreType.DMA((4,)),
        ],
        compiler_params=pltpu.CompilerParams(vmem_limit_bytes=58 << 20),
        cost_estimate=pl.CostEstimate(
            flops=40_000_000, bytes_accessed=12_000_000, transcendentals=0
        ),
        name="prepare",
    )(active, source, knockdown, cosine)


def solve_kernel(
    packed_ref, planes_hbm, slot_ref, slot_row_ref, total, out_ref,
    planes, slots, hit, bound, work, resid, side_y, side_x, tall, sems,
    *, peers, slot_depth, side,
):
    cases, cells_x, subs, width = total.shape
    parts = [slice(4, 6 + cases), slice(1, 3), slice(0, 1), slice(3, 4)]
    copies = [
        pltpu.make_async_copy(planes_hbm.at[part], planes.at[part], sems.at[k])
        for k, part in enumerate(parts)
    ]
    for copy in copies:
        copy.start()
    face_x, face_y, face_p, diag, inverse, along_y = (planes.at[k] for k in range(6))
    tiles = width // LANES
    lane = lax.broadcasted_iota(jnp.int32, (subs, LANES), 1)
    y_place = lane % side
    cut = [slice(t * LANES, (t + 1) * LANES) for t in range(tiles)]

    zero = jnp.zeros((subs, width), F32)
    for k in range(2):
        for c in range(cases):
            work[k, c, 0] = zero
            work[k, c, cells_x + 1] = zero

    unpack_slots(packed_ref, slots, peers, slot_depth)
    pieces = jnp.concatenate(split_two(slots[...]), axis=1)
    slot_lane = lax.broadcasted_iota(jnp.int32, (subs, peers * slot_depth), 1)
    for pair in range(2 * side):
        both = [
            jnp.where(slot_lane == slot_ref[:, q : q + 1], 1.0, 0.0)
            for q in (2 * pair, 2 * pair + 1)
        ]
        hit[pair * 2 * subs : (pair + 1) * 2 * subs, :] = jnp.concatenate(both, axis=0).astype(BF16)
    found = jnp.dot(hit[...], pieces, preferred_element_type=F32)
    rows = side * subs
    lower = lax.broadcasted_iota(jnp.int32, (4 * rows, LANES), 1) < HALF
    high, low = found[:, :LANES], found[:, LANES:]
    bound[0] = jnp.where(lower, high, pltpu.roll(low, HALF, 1)).astype(BF16)
    bound[1] = jnp.where(lower, pltpu.roll(high, HALF, 1), low).astype(BF16)

    ends_x = jnp.concatenate([bound[c, : 2 * rows, :] for c in range(cases)], axis=0)
    ends_y = jnp.concatenate(
        [
            jnp.concatenate([bound[c, 2 * rows : 3 * rows, :], bound[c, 3 * rows :, :]], axis=1)
            for c in range(cases)
        ],
        axis=0,
    )
    spread_x = indicator(ply_spread(LANES, width, side)[2])
    row, y_cell, own = ply_spread(2 * LANES, width, side)
    spread_y = indicator(own & (y_cell == jnp.where(row < LANES, 0, side - 1)))
    spread = jnp.dot(ends_x, spread_x, preferred_element_type=F32)
    side_y[...] = jnp.dot(ends_y, spread_y, preferred_element_type=F32)
    for c in range(cases):
        for e in range(2):
            base = (2 * c + e) * rows
            for t in range(tiles):
                gathered = spread[base : base + subs, cut[t]]
                for q in range(1, side):
                    part = spread[base + q * subs : base + (q + 1) * subs, cut[t]]
                    gathered = jnp.where(y_place == q, part, gathered)
                side_x[c, e, :, cut[t]] = gathered
    copies[0].wait()
    copies[1].wait()

    def residual(x, carry):
        at_first = jnp.where(x == 0, 1.0, 0.0)
        at_final = jnp.where(x == cells_x - 1, 1.0, 0.0)
        row = pl.multiple_of(x * subs, subs)
        for c in range(cases):
            for t in range(tiles):
                value = (
                    planes[6 + c, x, :, cut[t]]
                    + along_y[x, :, cut[t]] * side_y[pl.ds(c * rows + row, subs), cut[t]]
                    + at_first * (planes[1, cells_x, :, cut[t]] * side_x[c, 0, :, cut[t]])
                    + at_final * (planes[2, cells_x, :, cut[t]] * side_x[c, 1, :, cut[t]])
                )
                resid[c, x, :, cut[t]] = value
                work[0, c, x + 1, :, cut[t]] = (value * inverse[x, :, cut[t]]) * (1.0 / CHEB_CENTER)
        return carry

    lax.fori_loop(0, cells_x, residual, 0, unroll=4)
    copies[2].wait()
    copies[3].wait()

    def operate(x, c, old):
        w = [work[old, c, x + 1, :, cut[t]] for t in range(tiles)]
        fp = [face_p[x, :, cut[t]] for t in range(tiles)]
        below = from_lower_ply([fp[t] * w[t] for t in range(tiles)], side)
        above = from_upper_ply(w, side)
        out = []
        for t in range(tiles):
            fy = face_y[x, :, cut[t]]
            beside = (
                face_x[x, :, cut[t]] * work[old, c, x, :, cut[t]]
                + face_x[x + 1, :, cut[t]] * work[old, c, x + 2, :, cut[t]]
                + pltpu.roll(fy * w[t], 1, 1)
                + fy * pltpu.roll(w[t], LANES - 1, 1)
                + (below[t] + fp[t] * above[t])
            )
            out.append(diag[x, :, cut[t]] * w[t] - beside)
        return w, out

    sigma = CHEB_CENTER / CHEB_HALF
    rho_first = 1.0 / sigma
    rho_next = 1.0 / (2.0 * sigma - rho_first)
    keep = rho_next * rho_first
    gain = 2.0 * rho_next / CHEB_HALF

    for sweep in range(SWEEPS):
        final = sweep == SWEEPS - 1

        def second(x, carry, sweep=sweep, final=final):
            for c in range(cases):
                w, moved = operate(x, c, 0)
                for t in range(tiles):
                    r = resid[c, x, :, cut[t]] - moved[t]
                    later = keep * w[t] + gain * (r * inverse[x, :, cut[t]])
                    sums = w[t] + later
                    if sweep:
                        sums = total[c, x, :, cut[t]] + sums
                    total[c, x, :, cut[t]] = sums
                    if not final:
                        resid[c, x, :, cut[t]] = r
                        work[1, c, x + 1, :, cut[t]] = later
                    else:
                        row = pl.multiple_of(x * subs, subs)
                        side_y[pl.ds(c * rows + row, subs), cut[t]] = along_y[x, :, cut[t]] * (
                            side_y[pl.ds(c * rows + row, subs), cut[t]] - sums
                        )
            return carry

        lax.fori_loop(0, cells_x, second, 0, unroll=True)
        if final:
            break

        def first(x, carry):
            for c in range(cases):
                _, moved = operate(x, c, 1)
                for t in range(tiles):
                    r = resid[c, x, :, cut[t]] - moved[t]
                    resid[c, x, :, cut[t]] = r
                    work[0, c, x + 1, :, cut[t]] = (r * inverse[x, :, cut[t]]) * (1.0 / CHEB_CENTER)
            return carry

        lax.fori_loop(0, cells_x, first, 0, unroll=True)

    y_wide = lax.broadcasted_iota(jnp.int32, (subs, width), 1) % side
    for c in range(cases):
        for e, x in enumerate((0, cells_x - 1)):
            at_ply = planes[1 + e, cells_x] * (side_x[c, e] - total[c, x])
            for k, piece in enumerate(split_two(at_ply)):
                wide = piece.astype(F32)
                at = ((2 * c + e) * 2 + k) * rows
                tall[at : at + rows, :] = jnp.concatenate(
                    [jnp.where(y_wide == q, wide, 0.0) for q in range(side)], axis=0
                ).astype(BF16)
    across_lanes = (((1,), (1,)), ((), ()))
    folded_x = lax.dot_general(tall[...], spread_x, across_lanes, preferred_element_type=F32)
    folded_y = lax.dot_general(
        jnp.concatenate(split_two(side_y[...]), axis=0),
        spread_y,
        across_lanes,
        preferred_element_type=F32,
    )
    folded_y = folded_y[: cases * rows] + folded_y[cases * rows :]
    sums = []
    for c in range(cases):
        own = [
            folded_x[4 * c * rows + 2 * e * rows : 4 * c * rows + (2 * e + 1) * rows]
            + folded_x[4 * c * rows + (2 * e + 1) * rows : 4 * c * rows + (2 * e + 2) * rows]
            for e in range(2)
        ]
        part = folded_y[c * rows : (c + 1) * rows]
        sums.append(own + [part[:, :LANES], part[:, LANES:]])
    both = [jnp.where(lower[:rows], sums[0][e], sums[1][e]) for e in range(4)]
    forces = jnp.concatenate(
        [jnp.concatenate(split_two(part), axis=1) for part in both], axis=0
    )
    turned_hit = indicator(
        lax.broadcasted_iota(jnp.int32, (peers * slot_depth, 4 * rows), 0) == slot_row_ref[...]
    )
    posted = jnp.dot(turned_hit, forces, preferred_element_type=F32)
    slots[...] = posted[:, :LANES] + posted[:, LANES:]
    pack_slots(slots, out_ref, peers, slot_depth)


def solve_block(packed, ready, slot_index, source, peers, slot_depth, side):
    cases, subs, cells_x, width = source.shape
    points = slot_index.shape[1]
    vm = pl.BlockSpec(memory_space=pltpu.VMEM)
    hbm = pl.BlockSpec(memory_space=pltpu.HBM)
    out_rows = peers * packed_rows(slot_depth)
    planes = (cells_x, subs, width)
    return pl.pallas_call(
        functools.partial(solve_kernel, peers=peers, slot_depth=slot_depth, side=side),
        out_shape=(
            jax.ShapeDtypeStruct((cases,) + planes, F32),
            jax.ShapeDtypeStruct((out_rows, LANES), F32),
        ),
        in_specs=[vm, hbm, vm, vm],
        out_specs=(vm, vm),
        scratch_shapes=[
            pltpu.VMEM(ready.shape, F32),
            pltpu.VMEM((peers * slot_depth, LANES), F32),
            pltpu.VMEM((points * subs, peers * slot_depth), BF16),
            pltpu.VMEM((cases, 4 * side * subs, LANES), BF16),
            pltpu.VMEM((2, cases, cells_x + 2, subs, width), F32),
            pltpu.VMEM((cases,) + planes, F32),
            pltpu.VMEM((cases * side * subs, width), F32),
            pltpu.VMEM((cases, 2, subs, width), F32),
            pltpu.VMEM((4 * cases * side * subs, width), BF16),
            pltpu.SemaphoreType.DMA((4,)),
        ],
        compiler_params=pltpu.CompilerParams(vmem_limit_bytes=51 << 20),
        name="solve_block",
    )(packed, ready, slot_index, slot_index.T.reshape(1, points * subs))


def finish_kernel(total_ref, adjoint_ref, turned, *, side):
    cases, cells_x, subs, width = total_ref.shape
    rows = cases * cells_x * subs
    value = total_ref[...].reshape(rows, width)
    high = value.astype(BF16)
    rest = value - high.astype(F32)
    middle, low = split_two(rest)
    cell = lax.broadcasted_iota(jnp.int32, (width, width), 0)
    natural = lax.broadcasted_iota(jnp.int32, (width, width), 1)
    order = indicator(natural == ply_of(cell, width, side) * side + cell % side)
    found = jnp.dot(
        jnp.concatenate([high, middle, low], axis=0), order, preferred_element_type=F32
    )
    found = (found[:rows] + found[rows : 2 * rows]) + found[2 * rows :]
    for t in range(width // LANES):
        cut = slice(t * LANES, (t + 1) * LANES)
        for c in range(cases):
            for x in range(cells_x):
                at = (c * cells_x + x) * subs
                turned[t, pl.ds(c * subs * cells_x + x, subs, stride=cells_x), :] = found[
                    at : at + subs, cut
                ]
        adjoint_ref[:, cut] = turned[t]


def finish(total, side):
    cases, cells_x, subs, width = total.shape
    rows = cases * cells_x * subs
    vm = pl.BlockSpec(memory_space=pltpu.VMEM)
    adjoint = pl.pallas_call(
        functools.partial(finish_kernel, side=side),
        out_shape=jax.ShapeDtypeStruct((rows, width), F32),
        in_specs=[vm],
        out_specs=vm,
        scratch_shapes=[pltpu.VMEM((width // LANES, rows, LANES), F32)],
        compiler_params=pltpu.CompilerParams(vmem_limit_bytes=24 << 20),
        cost_estimate=pl.CostEstimate(
            flops=10_000_000, bytes_accessed=8_000_000, transcendentals=0
        ),
        name="finish",
    )(total)
    return adjoint.reshape(cases, subs, cells_x, width)


def per_device(shell_state, source, knockdown, orient, active, point_owner, owner_nodes):
    cases, subs, side_x, width = source.shape
    plies = orient.shape[1]
    side = width // plies
    node_local = shell_state.shape[2]
    _, peers, slot_depth = owner_nodes.shape
    axes = ("grp", "sub")
    per_peer = packed_rows(slot_depth)

    nodes = owner_nodes.reshape(peers, slot_depth)
    picked = gather_shell(shell_state.reshape(cases * plies, node_local), nodes)
    arrived = lax.all_to_all(
        picked.reshape(peers, per_peer, LANES), axes, split_axis=0, concat_axis=0, tiled=True
    )

    owners = point_owner.reshape(-1)
    place = jnp.arange(owners.shape[0])
    earlier = (owners[:, None] == owners[None, :]) & (place[None, :] < place[:, None])
    rank = jnp.sum(earlier.astype(jnp.int32), axis=1).reshape(point_owner.shape)
    slot_index = point_owner * slot_depth + rank
    ready = prepare(source, knockdown, orient, active)
    planes, outbound = solve_block(
        arrived.reshape(peers * per_peer, LANES), ready, slot_index, source, peers, slot_depth, side
    )
    returned = lax.all_to_all(
        outbound.reshape(peers, per_peer, LANES), axes, split_axis=0, concat_axis=0, tiled=True
    )
    late_nodes, planes = lax.optimization_barrier((nodes, planes))
    adjoint = finish(planes, side)
    same = pair_slots(late_nodes)
    node_rows = late_nodes.reshape(-1) + 8
    force = scatter_forces(
        returned.reshape(peers * per_peer, LANES), same, node_rows, peers, slot_depth,
        cases * plies, node_local,
    )
    return adjoint, force.reshape(cases, plies, node_local)


def solution(mesh):
    in_specs = (
        P(None, None, ("grp", "sub")),
        P(None, ("grp", "sub"), None, None),
        P(("grp", "sub"), None, None),
        P(("grp", "sub"), None),
        P(("grp", "sub")),
        P(("grp", "sub"), None),
        P(("grp", "sub"), None, None),
    )
    out_specs = (P(None, ("grp", "sub"), None, None), P(None, None, ("grp", "sub")))
    return jax.shard_map(
        per_device, mesh=mesh, in_specs=in_specs, out_specs=out_specs, check_vma=False
    )
```

```python
import functools
import math

import jax
import jax.numpy as jnp
from jax import lax
from jax.experimental import pallas as pl
from jax.experimental.pallas import tpu as pltpu
from jax.sharding import PartitionSpec as P

SWEEPS = 3
STEPS = 2

FIBER_COND = 1.0
TRANSVERSE = 0.25
THROUGH = 0.15
MASS_SHARE = 0.05
CHEB_CENTER = 1.02
CHEB_HALF = 0.98

LANES = 128
HALF = 64
F32 = jnp.float32
BF16 = jnp.bfloat16


def packed_rows(slot_depth):
    return slot_depth * 3 // 4 if slot_depth % 32 == 0 else slot_depth


def pack_slots(rows_ref, out_ref, peers, slot_depth):
    used = lax.broadcasted_iota(jnp.int32, (8, LANES), 1) % HALF < 48
    if slot_depth % 32:
        for g in range(peers * slot_depth // 8):
            part = slice(g * 8, g * 8 + 8)
            out_ref[part, :] = jnp.where(used, rows_ref[part, :], 0.0)
        return
    for g in range(peers * slot_depth // 32):
        extra = rows_ref[g * 32 + 24 : g * 32 + 32, :]
        for k in range(3):
            moved = pltpu.roll(extra, 48 - 16 * k, 1)
            own = rows_ref[g * 32 + 8 * k : g * 32 + 8 * k + 8, :]
            out_ref[g * 24 + 8 * k : g * 24 + 8 * k + 8, :] = jnp.where(used, own, moved)


def unpack_slots(packed_ref, rows_ref, peers, slot_depth):
    if slot_depth % 32:
        rows_ref[...] = packed_ref[...]
        return
    third = lax.broadcasted_iota(jnp.int32, (8, LANES), 1) % HALF // 16
    for g in range(peers * slot_depth // 32):
        parts = []
        for k in range(3):
            own = packed_ref[g * 24 + 8 * k : g * 24 + 8 * k + 8, :]
            rows_ref[g * 32 + 8 * k : g * 32 + 8 * k + 8, :] = own
            parts.append(pltpu.roll(own, LANES - 48 + 16 * k, 1))
        extra = jnp.where(third == 0, parts[0], jnp.where(third == 1, parts[1], parts[2]))
        rows_ref[g * 32 + 24 : g * 32 + 32, :] = extra


def split_two(value):
    high = value.astype(BF16)
    return high, (value - high.astype(F32)).astype(BF16)


def indicator(condition):
    return jnp.where(condition, 1.0, 0.0).astype(BF16)


def gather_kernel(
    node_ref, shell_hbm, out_hbm, shell, turned, rows, packed, sems, out_sems, *, peers, slot_depth
):
    width, node_local = shell.shape
    chunks = sems.shape[0]
    chunk = node_local // chunks
    copies = []
    for i in range(chunks):
        part = slice(i * chunk, (i + 1) * chunk)
        copies.append(pltpu.make_async_copy(shell_hbm.at[:, part], shell.at[:, part], sems.at[i]))
        copies[i].start()
    gap = jnp.zeros((HALF - width // 2, LANES), F32)
    gap_two = jnp.zeros((HALF - width // 2, 2 * LANES), F32)
    unit_row = lax.broadcasted_iota(jnp.int32, (2 * LANES, 2 * LANES), 0)
    unit = indicator(unit_row == lax.broadcasted_iota(jnp.int32, (2 * LANES, 2 * LANES), 1))
    across_lanes = (((1,), (1,)), ((), ()))
    tiles = chunk // LANES
    in_matmul = tiles // 8 * 2
    for i in range(chunks):
        copies[i].wait()
        for t in range(i * tiles, i * tiles + in_matmul, 2):
            tile = shell[:, t * LANES : (t + 2) * LANES]
            both = jnp.concatenate(
                [tile[: width // 2], gap_two, tile[width // 2 :], gap_two], axis=0
            )
            pieces = jnp.concatenate(split_two(both), axis=0)
            out = lax.dot_general(unit, pieces, across_lanes, preferred_element_type=F32)
            turned[8 + t * LANES : 8 + (t + 2) * LANES, :] = out[:, :LANES] + out[:, LANES:]
        for t in range(i * tiles + in_matmul, (i + 1) * tiles):
            tile = shell[:, t * LANES : (t + 1) * LANES]
            parts = [tile[: width // 2], gap, tile[width // 2 :], gap]
            turned[8 + t * LANES : 8 + (t + 1) * LANES, :] = jnp.concatenate(parts, axis=0).T
    turned[0:8, :] = turned[8:16, :]

    def pick(peer, carry):
        for u in range(slot_depth):
            slot = peer * slot_depth + u
            rows[pl.ds(slot, 1), :] = turned[pl.ds(node_ref[peer, u] + 8, 1), :]
        return carry

    groups = out_sems.shape[0]
    share = peers // groups
    per_peer = packed_rows(slot_depth)
    sends = []
    for g in range(groups):
        lax.fori_loop(g * share, (g + 1) * share, pick, 0, unroll=4)
        own = slice(g * share * slot_depth, (g + 1) * share * slot_depth)
        part = slice(g * share * per_peer, (g + 1) * share * per_peer)
        pack_slots(rows.at[own], packed.at[part], share, slot_depth)
        sends.append(pltpu.make_async_copy(packed.at[part], out_hbm.at[part], out_sems.at[g]))
        sends[g].start()
    for send in sends:
        send.wait()


def gather_shell(shell_flat, nodes):
    width, node_local = shell_flat.shape
    peers, slot_depth = nodes.shape
    chunks, groups = 4, 8
    out_rows = peers * packed_rows(slot_depth)
    return pl.pallas_call(
        functools.partial(gather_kernel, peers=peers, slot_depth=slot_depth),
        out_shape=jax.ShapeDtypeStruct((out_rows, LANES), F32),
        in_specs=[
            pl.BlockSpec(memory_space=pltpu.SMEM),
            pl.BlockSpec(memory_space=pltpu.HBM),
        ],
        out_specs=pl.BlockSpec(memory_space=pltpu.HBM),
        scratch_shapes=[
            pltpu.VMEM((width, node_local), F32),
            pltpu.VMEM((node_local + 8, LANES), F32),
            pltpu.VMEM((peers * slot_depth, LANES), F32),
            pltpu.VMEM((out_rows, LANES), F32),
            pltpu.SemaphoreType.DMA((chunks,)),
            pltpu.SemaphoreType.DMA((groups,)),
        ],
        name="gather_shell",
    )(nodes, shell_flat)


def pair_kernel(node_turned_ref, node_row_ref, same_ref):
    depth, peers = node_turned_ref.shape
    for peer in range(peers):
        column = node_turned_ref[:, peer : peer + 1]
        same_ref[peer * depth : (peer + 1) * depth, :] = jnp.where(
            column == node_row_ref[...], 1.0, 0.0
        ).astype(BF16)


def pair_slots(nodes):
    peers, slot_depth = nodes.shape
    slots = peers * slot_depth
    vm = pl.BlockSpec(memory_space=pltpu.VMEM)
    return pl.pallas_call(
        pair_kernel,
        out_shape=jax.ShapeDtypeStruct((slots, slots), BF16),
        in_specs=[vm] * 2,
        out_specs=vm,
        compiler_params=pltpu.CompilerParams(vmem_limit_bytes=16 << 20),
        cost_estimate=pl.CostEstimate(
            flops=4_000_000, bytes_accessed=4_000_000, transcendentals=0
        ),
        name="pair_slots",
    )(nodes.T, nodes.reshape(1, slots))


def scatter_kernel(
    row_ref, same_ref, packed_ref, out_hbm, total, rows, out, sems, *, peers, slot_depth
):
    width, node_local = out.shape
    unpack_slots(packed_ref, rows, peers, slot_depth)
    pieces = jnp.concatenate(split_two(rows[...]), axis=1)
    zero = jnp.zeros((LANES, LANES), F32)
    for t in range(node_local // LANES):
        total[8 + t * LANES : 8 + (t + 1) * LANES, :] = zero
    summed = jnp.dot(same_ref[...], pieces, preferred_element_type=F32)
    rows[...] = summed[:, :LANES] + summed[:, LANES:]

    def put(group, carry):
        for u in range(LANES):
            slot = group * LANES + u
            total[pl.ds(row_ref[slot], 1), :] = rows[pl.ds(slot, 1), :]
        return carry

    lax.fori_loop(0, peers * slot_depth // LANES, put, 0)

    chunks = sems.shape[0]
    chunk = node_local // chunks
    copies = []
    for i in range(chunks):
        for t in range(i * chunk // LANES, (i + 1) * chunk // LANES):
            tile = total[8 + t * LANES : 8 + (t + 1) * LANES, :].T
            out[: width // 2, t * LANES : (t + 1) * LANES] = tile[: width // 2]
            out[width // 2 :, t * LANES : (t + 1) * LANES] = tile[HALF : HALF + width // 2]
        part = slice(i * chunk, (i + 1) * chunk)
        copies.append(pltpu.make_async_copy(out.at[:, part], out_hbm.at[:, part], sems.at[i]))
        copies[i].start()
    for copy in copies:
        copy.wait()


def scatter_forces(packed, same, node_rows, peers, slot_depth, width, node_local):
    chunks = 8
    vm = pl.BlockSpec(memory_space=pltpu.VMEM)
    return pl.pallas_call(
        functools.partial(scatter_kernel, peers=peers, slot_depth=slot_depth),
        out_shape=jax.ShapeDtypeStruct((width, node_local), F32),
        in_specs=[pl.BlockSpec(memory_space=pltpu.SMEM), vm, vm],
        out_specs=pl.BlockSpec(memory_space=pltpu.HBM),
        scratch_shapes=[
            pltpu.VMEM((node_local + 8, LANES), F32),
            pltpu.VMEM((peers * slot_depth, LANES), F32),
            pltpu.VMEM((width, node_local), F32),
            pltpu.SemaphoreType.DMA((chunks,)),
        ],
        compiler_params=pltpu.CompilerParams(vmem_limit_bytes=40 << 20),
        name="scatter_forces",
    )(node_rows, same, packed)


def ply_of(cell, width, side):
    return cell % LANES // side * (width // LANES) + cell // LANES


def from_lower_ply(values, side):
    return [pltpu.roll(values[-1], side, 1)] + values[:-1]


def from_upper_ply(values, side):
    return values[1:] + [pltpu.roll(values[0], LANES - side, 1)]


def ply_spread(tall, width, side):
    row = lax.broadcasted_iota(jnp.int32, (tall, width), 0)
    cell = lax.broadcasted_iota(jnp.int32, (tall, width), 1)
    return row, cell % side, row % HALF == ply_of(cell, width, side)


def prepare_kernel(
    active_ref, source_ref, knock_ref, cosine_ref, slot_ref, planes_hbm, hit,
    planes, src, knock, ply_ref, sems, *, plies, side,
):
    cases, subs, cells_x, width = source_ref.shape
    tiles = width // LANES
    lane = lax.broadcasted_iota(jnp.int32, (subs, LANES), 1)
    y_place = lane % side
    first_y = y_place == 0
    last_y = y_place == side - 1
    cut = [slice(t * LANES, (t + 1) * LANES) for t in range(tiles)]

    slot_lane = lax.broadcasted_iota(jnp.int32, (subs, hit.shape[1]), 1)
    for pair in range(2 * side):
        both = [
            jnp.where(slot_lane == slot_ref[:, q : q + 1], 1.0, 0.0)
            for q in (2 * pair, 2 * pair + 1)
        ]
        hit[pair * 2 * subs : (pair + 1) * 2 * subs, :] = jnp.concatenate(both, axis=0).astype(BF16)

    ply = lax.broadcasted_iota(jnp.int32, (subs, plies), 1)
    sub = lax.broadcasted_iota(jnp.int32, (subs, plies), 0)
    present = jnp.zeros((subs, plies), jnp.int32)
    for s in range(subs):
        present = jnp.where(sub == s, active_ref[s], present)
    mask = jnp.where(ply < present, 1.0, 0.0)
    upper = jnp.where((ply + 1 < present) & (ply + 1 < plies), 0.5, 0.0)
    cos_square = cosine_ref[...]
    terms = jnp.concatenate(
        [
            (FIBER_COND * cos_square + TRANSVERSE * (1.0 - cos_square)) * mask,
            (FIBER_COND * (1.0 - cos_square) + TRANSVERSE * cos_square) * mask,
            mask,
            upper,
        ],
        axis=0,
    )
    high, low = split_two(terms)
    only = indicator(ply_spread(plies, width, side)[2])
    spread_terms = jnp.dot(high, only, preferred_element_type=F32) + jnp.dot(
        low, only, preferred_element_type=F32
    )
    for k in range(4):
        ply_ref[k] = spread_terms[k * subs : (k + 1) * subs, :]

    natural = lax.broadcasted_iota(jnp.int32, (width, width), 0)
    cell = lax.broadcasted_iota(jnp.int32, (width, width), 1)
    order = indicator(natural == ply_of(cell, width, side) * side + cell % side)
    for ref, into in ((source_ref, src), (knock_ref, knock)):
        ordered = jnp.dot(ref[...].reshape(-1, width), order, preferred_element_type=F32)
        for t in range(tiles):
            into[t] = ordered[:, cut[t]]

    def plane(ref, x, base=0):
        return [ref[t, pl.ds(base + x, subs, stride=cells_x), :] for t in range(tiles)]

    face_x, face_y, face_p, inverse, along_y = (planes.at[k] for k in range(5))
    face_x[0] = jnp.zeros((subs, width), F32)
    face_x[cells_x] = jnp.zeros((subs, width), F32)

    def faces_x(x, carry):
        here = plane(knock, x)
        there = plane(knock, x + 1)
        for t in range(tiles):
            fiber = ply_ref[0, :, cut[t]]
            face_x[x + 1, :, cut[t]] = 0.5 * (here[t] * fiber + there[t] * fiber)
        return carry

    lax.fori_loop(0, cells_x - 1, faces_x, 0, unroll=5)

    def coefficients(x, carry):
        k = plane(knock, x)
        ax = [k[t] * ply_ref[0, :, cut[t]] for t in range(tiles)]
        ay = [k[t] * ply_ref[1, :, cut[t]] for t in range(tiles)]
        ac = [k[t] * (THROUGH * ply_ref[2, :, cut[t]]) for t in range(tiles)]
        up = from_upper_ply(ac, side)
        fp = [ply_ref[3, :, cut[t]] * (ac[t] + up[t]) for t in range(tiles)]
        below = from_lower_ply(fp, side)
        at_edge = jnp.where((x == 0) | (x == cells_x - 1), 1.0, 0.0)
        for t in range(tiles):
            fy = jnp.where(last_y, 0.0, 0.5 * (ay[t] + pltpu.roll(ay[t], LANES - 1, 1)))
            whole = (
                face_x[x, :, cut[t]]
                + face_x[x + 1, :, cut[t]]
                + pltpu.roll(fy, 1, 1)
                + fy
                + below[t]
                + fp[t]
                + at_edge * ax[t]
                + jnp.where(first_y | last_y, ay[t], 0.0)
                + MASS_SHARE * (ax[t] + ay[t] + ac[t])
                + (1.0 - ply_ref[2, :, cut[t]])
            )
            face_y[x, :, cut[t]] = fy
            face_p[x, :, cut[t]] = fp[t]
            inverse[x, :, cut[t]] = 1.0 / whole
            along_y[x, :, cut[t]] = ay[t]
            for c in range(cases):
                value = src[t, pl.ds(c * subs * cells_x + x, subs, stride=cells_x), :]
                planes[5 + c, x, :, cut[t]] = ply_ref[2, :, cut[t]] * value
        return carry

    for e, x in enumerate((0, cells_x - 1)):
        k = plane(knock, x)
        for t in range(tiles):
            planes[3 + e, cells_x, :, cut[t]] = k[t] * ply_ref[0, :, cut[t]]
    bands = sems.shape[0]
    band = cells_x // bands
    copies = []
    for i in range(bands):
        lax.fori_loop(i * band, (i + 1) * band, coefficients, 0, unroll=True)
        part = pl.ds(i * band, band + (1 if i == bands - 1 else 0))
        copies.append(
            pltpu.make_async_copy(planes.at[:, part], planes_hbm.at[:, part], sems.at[i])
        )
        copies[i].start()
    for copy in copies:
        copy.wait()


def prepare(source, knockdown, orient, active, slot_index, slots):
    cases, subs, cells_x, width = source.shape
    plies = orient.shape[1]
    side = width // plies
    cosine = jnp.cos(orient.astype(F32) * (math.pi / 6.0)) ** 2
    planes = (5 + cases, cells_x + 1, subs, width)
    vm = pl.BlockSpec(memory_space=pltpu.VMEM)
    return pl.pallas_call(
        functools.partial(prepare_kernel, plies=plies, side=side),
        out_shape=(
            jax.ShapeDtypeStruct(planes, F32),
            jax.ShapeDtypeStruct((slot_index.size, slots), BF16),
        ),
        in_specs=[pl.BlockSpec(memory_space=pltpu.SMEM)] + [vm] * 4,
        out_specs=(pl.BlockSpec(memory_space=pltpu.HBM), vm),
        scratch_shapes=[
            pltpu.VMEM(planes, F32),
            pltpu.VMEM((width // LANES, cases * subs * cells_x, LANES), F32),
            pltpu.VMEM((width // LANES, subs * cells_x, LANES), F32),
            pltpu.VMEM((4, subs, width), F32),
            pltpu.SemaphoreType.DMA((4,)),
        ],
        compiler_params=pltpu.CompilerParams(vmem_limit_bytes=52 << 20),
        cost_estimate=pl.CostEstimate(
            flops=40_000_000, bytes_accessed=12_000_000, transcendentals=0
        ),
        name="prepare",
    )(active, source, knockdown, cosine, slot_index)


def solve_kernel(
    packed_ref, planes_hbm, hit_ref, slot_row_ref, total, out_ref,
    planes, slots, bound, work, resid, side_y, side_x, tall, sems,
    *, peers, slot_depth, side,
):
    cases, cells_x, subs, width = total.shape
    parts = [slice(3, 5 + cases), slice(0, 3)]
    copies = [
        pltpu.make_async_copy(planes_hbm.at[part], planes.at[part], sems.at[k])
        for k, part in enumerate(parts)
    ]
    for copy in copies:
        copy.start()
    face_x, face_y, face_p, inverse, along_y = (planes.at[k] for k in range(5))
    tiles = width // LANES
    lane = lax.broadcasted_iota(jnp.int32, (subs, LANES), 1)
    y_place = lane % side
    cut = [slice(t * LANES, (t + 1) * LANES) for t in range(tiles)]

    zero = jnp.zeros((subs, width), F32)
    for k in range(2):
        for c in range(cases):
            work[k, c, 0] = zero
            work[k, c, cells_x + 1] = zero

    unpack_slots(packed_ref, slots, peers, slot_depth)
    pieces = jnp.concatenate(split_two(slots[...]), axis=1)
    found = jnp.dot(hit_ref[...], pieces, preferred_element_type=F32)
    rows = side * subs
    lower = lax.broadcasted_iota(jnp.int32, (4 * rows, LANES), 1) < HALF
    high, low = found[:, :LANES], found[:, LANES:]
    bound[0] = jnp.where(lower, high, pltpu.roll(low, HALF, 1)).astype(BF16)
    bound[1] = jnp.where(lower, pltpu.roll(high, HALF, 1), low).astype(BF16)

    ends_x = jnp.concatenate([bound[c, : 2 * rows, :] for c in range(cases)], axis=0)
    ends_y = jnp.concatenate(
        [
            jnp.concatenate([bound[c, 2 * rows : 3 * rows, :], bound[c, 3 * rows :, :]], axis=1)
            for c in range(cases)
        ],
        axis=0,
    )
    spread_x = indicator(ply_spread(LANES, width, side)[2])
    row, y_cell, own = ply_spread(2 * LANES, width, side)
    spread_y = indicator(own & (y_cell == jnp.where(row < LANES, 0, side - 1)))
    spread = jnp.dot(ends_x, spread_x, preferred_element_type=F32)
    side_y[...] = jnp.dot(ends_y, spread_y, preferred_element_type=F32)
    for c in range(cases):
        for e in range(2):
            base = (2 * c + e) * rows
            for t in range(tiles):
                gathered = spread[base : base + subs, cut[t]]
                for q in range(1, side):
                    part = spread[base + q * subs : base + (q + 1) * subs, cut[t]]
                    gathered = jnp.where(y_place == q, part, gathered)
                side_x[c, e, :, cut[t]] = gathered
    copies[0].wait()

    def residual(x, carry):
        at_first = jnp.where(x == 0, 1.0, 0.0)
        at_final = jnp.where(x == cells_x - 1, 1.0, 0.0)
        row = pl.multiple_of(x * subs, subs)
        for c in range(cases):
            for t in range(tiles):
                value = (
                    planes[5 + c, x, :, cut[t]]
                    + along_y[x, :, cut[t]] * side_y[pl.ds(c * rows + row, subs), cut[t]]
                    + at_first * (planes[3, cells_x, :, cut[t]] * side_x[c, 0, :, cut[t]])
                    + at_final * (planes[4, cells_x, :, cut[t]] * side_x[c, 1, :, cut[t]])
                )
                resid[c, x, :, cut[t]] = value
                work[0, c, x + 1, :, cut[t]] = (value * inverse[x, :, cut[t]]) * (1.0 / CHEB_CENTER)
        return carry

    lax.fori_loop(0, cells_x, residual, 0, unroll=4)
    copies[1].wait()

    def operate(x, c, old):
        w = [work[old, c, x + 1, :, cut[t]] for t in range(tiles)]
        fp = [face_p[x, :, cut[t]] for t in range(tiles)]
        below = from_lower_ply([fp[t] * w[t] for t in range(tiles)], side)
        above = from_upper_ply(w, side)
        out = []
        for t in range(tiles):
            fy = face_y[x, :, cut[t]]
            beside = (
                face_x[x, :, cut[t]] * work[old, c, x, :, cut[t]]
                + face_x[x + 1, :, cut[t]] * work[old, c, x + 2, :, cut[t]]
                + pltpu.roll(fy * w[t], 1, 1)
                + fy * pltpu.roll(w[t], LANES - 1, 1)
                + (below[t] + fp[t] * above[t])
            )
            out.append(beside)
        return w, out

    sigma = CHEB_CENTER / CHEB_HALF
    rho_first = 1.0 / sigma
    rho_next = 1.0 / (2.0 * sigma - rho_first)
    keep = rho_next * rho_first
    gain = 2.0 * rho_next / CHEB_HALF

    for sweep in range(SWEEPS):
        final = sweep == SWEEPS - 1

        def second(x, carry, sweep=sweep, final=final):
            for c in range(cases):
                w, beside = operate(x, c, 0)
                for t in range(tiles):
                    before = resid[c, x, :, cut[t]]
                    r = (1.0 - 1.0 / CHEB_CENTER) * before + beside[t]
                    later = keep * w[t] + gain * (r * inverse[x, :, cut[t]])
                    sums = w[t] + later
                    if sweep:
                        sums = total[c, x, :, cut[t]] + sums
                    total[c, x, :, cut[t]] = sums
                    if not final:
                        resid[c, x, :, cut[t]] = (1.0 - gain) * r - (keep / CHEB_CENTER) * before
                        work[1, c, x + 1, :, cut[t]] = later
                    else:
                        row = pl.multiple_of(x * subs, subs)
                        side_y[pl.ds(c * rows + row, subs), cut[t]] = along_y[x, :, cut[t]] * (
                            side_y[pl.ds(c * rows + row, subs), cut[t]] - sums
                        )
            return carry

        lax.fori_loop(0, cells_x, second, 0, unroll=True)
        if final:
            break

        def first(x, carry):
            for c in range(cases):
                _, beside = operate(x, c, 1)
                for t in range(tiles):
                    r = resid[c, x, :, cut[t]] + beside[t]
                    resid[c, x, :, cut[t]] = r
                    work[0, c, x + 1, :, cut[t]] = (r * inverse[x, :, cut[t]]) * (1.0 / CHEB_CENTER)
            return carry

        lax.fori_loop(0, cells_x, first, 0, unroll=True)

    y_wide = lax.broadcasted_iota(jnp.int32, (subs, width), 1) % side
    for c in range(cases):
        for e, x in enumerate((0, cells_x - 1)):
            at_ply = planes[3 + e, cells_x] * (side_x[c, e] - total[c, x])
            for k, piece in enumerate(split_two(at_ply)):
                wide = piece.astype(F32)
                at = ((2 * c + e) * 2 + k) * rows
                tall[at : at + rows, :] = jnp.concatenate(
                    [jnp.where(y_wide == q, wide, 0.0) for q in range(side)], axis=0
                ).astype(BF16)
    across_lanes = (((1,), (1,)), ((), ()))
    folded_x = lax.dot_general(tall[...], spread_x, across_lanes, preferred_element_type=F32)
    folded_y = lax.dot_general(
        jnp.concatenate(split_two(side_y[...]), axis=0),
        spread_y,
        across_lanes,
        preferred_element_type=F32,
    )
    folded_y = folded_y[: cases * rows] + folded_y[cases * rows :]
    sums = []
    for c in range(cases):
        own = [
            folded_x[4 * c * rows + 2 * e * rows : 4 * c * rows + (2 * e + 1) * rows]
            + folded_x[4 * c * rows + (2 * e + 1) * rows : 4 * c * rows + (2 * e + 2) * rows]
            for e in range(2)
        ]
        part = folded_y[c * rows : (c + 1) * rows]
        sums.append(own + [part[:, :LANES], part[:, LANES:]])
    both = [jnp.where(lower[:rows], sums[0][e], sums[1][e]) for e in range(4)]
    forces = jnp.concatenate(
        [jnp.concatenate(split_two(part), axis=1) for part in both], axis=0
    )
    turned_hit = indicator(
        lax.broadcasted_iota(jnp.int32, (peers * slot_depth, 4 * rows), 0) == slot_row_ref[...]
    )
    posted = jnp.dot(turned_hit, forces, preferred_element_type=F32)
    slots[...] = posted[:, :LANES] + posted[:, LANES:]
    pack_slots(slots, out_ref, peers, slot_depth)


def solve_block(packed, ready, hit, slot_index, source, peers, slot_depth, side):
    cases, subs, cells_x, width = source.shape
    points = slot_index.shape[1]
    vm = pl.BlockSpec(memory_space=pltpu.VMEM)
    hbm = pl.BlockSpec(memory_space=pltpu.HBM)
    out_rows = peers * packed_rows(slot_depth)
    planes = (cells_x, subs, width)
    return pl.pallas_call(
        functools.partial(solve_kernel, peers=peers, slot_depth=slot_depth, side=side),
        out_shape=(
            jax.ShapeDtypeStruct((cases,) + planes, F32),
            jax.ShapeDtypeStruct((out_rows, LANES), F32),
        ),
        in_specs=[vm, hbm, vm, vm],
        out_specs=(vm, vm),
        scratch_shapes=[
            pltpu.VMEM(ready.shape, F32),
            pltpu.VMEM((peers * slot_depth, LANES), F32),
            pltpu.VMEM((cases, 4 * side * subs, LANES), BF16),
            pltpu.VMEM((2, cases, cells_x + 2, subs, width), F32),
            pltpu.VMEM((cases,) + planes, F32),
            pltpu.VMEM((cases * side * subs, width), F32),
            pltpu.VMEM((cases, 2, subs, width), F32),
            pltpu.VMEM((4 * cases * side * subs, width), BF16),
            pltpu.SemaphoreType.DMA((2,)),
        ],
        compiler_params=pltpu.CompilerParams(vmem_limit_bytes=51 << 20),
        name="solve_block",
    )(packed, ready, hit, slot_index.T.reshape(1, points * subs))


def finish_kernel(total_ref, adjoint_ref, turned, *, side):
    cases, cells_x, subs, width = total_ref.shape
    rows = cases * cells_x * subs
    value = total_ref[...].reshape(rows, width)
    high = value.astype(BF16)
    rest = value - high.astype(F32)
    middle, low = split_two(rest)
    cell = lax.broadcasted_iota(jnp.int32, (width, width), 0)
    natural = lax.broadcasted_iota(jnp.int32, (width, width), 1)
    order = indicator(natural == ply_of(cell, width, side) * side + cell % side)
    found = jnp.dot(
        jnp.concatenate([high, middle, low], axis=0), order, preferred_element_type=F32
    )
    found = (found[:rows] + found[rows : 2 * rows]) + found[2 * rows :]
    for t in range(width // LANES):
        cut = slice(t * LANES, (t + 1) * LANES)
        for c in range(cases):
            for x in range(cells_x):
                at = (c * cells_x + x) * subs
                turned[t, pl.ds(c * subs * cells_x + x, subs, stride=cells_x), :] = found[
                    at : at + subs, cut
                ]
        adjoint_ref[:, cut] = turned[t]


def finish(total, side):
    cases, cells_x, subs, width = total.shape
    rows = cases * cells_x * subs
    vm = pl.BlockSpec(memory_space=pltpu.VMEM)
    adjoint = pl.pallas_call(
        functools.partial(finish_kernel, side=side),
        out_shape=jax.ShapeDtypeStruct((rows, width), F32),
        in_specs=[vm],
        out_specs=vm,
        scratch_shapes=[pltpu.VMEM((width // LANES, rows, LANES), F32)],
        compiler_params=pltpu.CompilerParams(vmem_limit_bytes=24 << 20),
        cost_estimate=pl.CostEstimate(
            flops=10_000_000, bytes_accessed=8_000_000, transcendentals=0
        ),
        name="finish",
    )(total)
    return adjoint.reshape(cases, subs, cells_x, width)


def per_device(shell_state, source, knockdown, orient, active, point_owner, owner_nodes):
    cases, subs, side_x, width = source.shape
    plies = orient.shape[1]
    side = width // plies
    node_local = shell_state.shape[2]
    _, peers, slot_depth = owner_nodes.shape
    axes = ("grp", "sub")
    per_peer = packed_rows(slot_depth)

    nodes = owner_nodes.reshape(peers, slot_depth)
    picked = gather_shell(shell_state.reshape(cases * plies, node_local), nodes)
    arrived = lax.all_to_all(
        picked.reshape(peers, per_peer, LANES), axes, split_axis=0, concat_axis=0, tiled=True
    )

    owners = point_owner.reshape(-1)
    place = jnp.arange(owners.shape[0])
    earlier = (owners[:, None] == owners[None, :]) & (place[None, :] < place[:, None])
    rank = jnp.sum(earlier.astype(jnp.int32), axis=1).reshape(point_owner.shape)
    slot_index = point_owner * slot_depth + rank
    ready, hit = prepare(
        source, knockdown, orient, active, slot_index, peers * slot_depth
    )
    planes, outbound = solve_block(
        arrived.reshape(peers * per_peer, LANES), ready, hit, slot_index, source, peers, slot_depth, side
    )
    returned = lax.all_to_all(
        outbound.reshape(peers, per_peer, LANES), axes, split_axis=0, concat_axis=0, tiled=True
    )
    late_nodes, planes = lax.optimization_barrier((nodes, planes))
    adjoint = finish(planes, side)
    same = pair_slots(late_nodes)
    node_rows = late_nodes.reshape(-1) + 8
    force = scatter_forces(
        returned.reshape(peers * per_peer, LANES), same, node_rows, peers, slot_depth,
        cases * plies, node_local,
    )
    return adjoint, force.reshape(cases, plies, node_local)


def solution(mesh):
    in_specs = (
        P(None, None, ("grp", "sub")),
        P(None, ("grp", "sub"), None, None),
        P(("grp", "sub"), None, None),
        P(("grp", "sub"), None),
        P(("grp", "sub")),
        P(("grp", "sub"), None),
        P(("grp", "sub"), None, None),
    )
    out_specs = (P(None, ("grp", "sub"), None, None), P(None, None, ("grp", "sub")))
    return jax.shard_map(
        per_device, mesh=mesh, in_specs=in_specs, out_specs=out_specs, check_vma=False
    )
```
